512 devices in a mesh: row: 32 (over y, x), col: 16 (over z, core).
Axes of the slice: x: 4, y: 8, z: 8, core: 2. Of those that a mesh axis runs over, the one named last changes fastest.
Arguments:
- gram_panel: float32 [8192, 1024], P('row', 'col'), may hold values from -2973.8 to 2973.8, as said below
- left_factor: bfloat16 [8192, 16384], P('row', 'col'), may hold values from -0.42426407 to 0.42426407
- solved_prev: bfloat16 [16384, 8192], P('row', 'col'), may hold values from -0.59765625 to 0.59765625
- right_block: float32 [1024, 8192], P('row', 'col'), may hold values from -6 to 6
Outputs:
- panel_factor: float32 [8192, 1024], P('row', 'col')
- solved_panel: float32 [1024, 8192], P('row', 'col')
The draws below stay inside these ranges and needn't reach their ends.
Inputs may be any that keep to these rules, and one draw needn't show every extreme that they name: The rows of gram_panel at the panel's indices minus the product of the corresponding rows of left_factor with their transpose form a symmetric positive definite matrix.
All inputs are finite; a program needn't handle non-finite values.
Results may differ from the reference program's by a relative error of at most 0.0006.
Values may be sent and summed in bfloat16 or wider, within the bound.
No kernel may reach another device: no remote copies, remote signals or barrier semaphores. Data moves between devices by JAX's collectives and lax.ppermute only.
A program may use at most 64 MiB of HBM per device.

```python
import jax
import jax.numpy as jnp
from jax import lax

PANEL = 1024
ROWS_DEV = 256
ROWS = 8192
PREV = 16384
VOX = 8192
BLOCK = 32
N_ROW = 32


def panel_index_drawn():
    grid = jnp.arange(N_ROW, dtype=jnp.int32)[:, None] * ROWS_DEV + jnp.arange(BLOCK, dtype=jnp.int32)[None, :]
    return grid.reshape(-1).astype(jnp.int32)


def left_values(key):
    source = jax.random.fold_in(key, 17)
    spread = 0.95 * PREV ** (-0.25)
    values = jnp.clip(jax.random.normal(source, (ROWS, PREV), jnp.float32), -5.0, 5.0) * spread
    return values.astype(jnp.bfloat16)


def draw_left_factor(key, part):
    return left_values(key)


def draw_gram_panel(key, part):
    left = left_values(key).astype(jnp.float32)
    chosen = left[panel_index_drawn()]
    cross = jnp.dot(chosen, chosen.T, precision=lax.Precision.HIGHEST)
    first = jax.random.fold_in(jax.random.fold_in(key, 29), 0)
    third = jax.random.fold_in(jax.random.fold_in(key, 29), 2)
    fourth = jax.random.fold_in(jax.random.fold_in(key, 29), 3)
    outer = jnp.clip(jax.random.normal(first, (ROWS, PANEL), jnp.float32), -6.0, 6.0) * 0.9
    basis = jnp.clip(jax.random.normal(third, (PANEL, PANEL), jnp.float32), -4.0, 4.0)
    mixed = jnp.dot(basis, basis.T, precision=lax.Precision.HIGHEST) / PANEL
    mixed = 0.5 * (mixed + mixed.T)
    ridge = jax.random.uniform(fourth, (PANEL,), jnp.float32, 0.1, 0.3)
    block = cross + mixed + jnp.diag(ridge)
    return outer.at[panel_index_drawn()].set(block)


def block_scale(own_key, extent, shards, least, top_value):
    def one(axis_at, blocks):
        steps = jax.random.uniform(jax.random.fold_in(jax.random.fold_in(own_key, 6), axis_at), (blocks,), jnp.float32, least / len(shards), top_value / len(shards))
        return jnp.repeat(jnp.exp(steps), extent[axis_at] // blocks).reshape((-1,) + (1,) * (len(extent) - axis_at - 1))

    loudness = one(*shards[0])
    for cut in shards[1:]:
        loudness = loudness * one(*cut)
    return loudness


def gaussian(rng, extent, scale, reach, pieces=(), held_as=jnp.bfloat16):
    array = jax.random.normal(rng, extent, jnp.float32) * scale
    if len(pieces) > 0:
        array = block_scale(rng, extent, pieces, -0.22, 0.18) * array
    return jnp.clip(array, min=-reach, max=reach).astype(held_as)


def setup_inputs(seed: int = 0) -> dict:
    seeds = jax.random.split(jax.random.key(seed), 5)
    gram_panel = draw_gram_panel(jax.random.fold_in(seeds[4], 71), 0)
    left_factor = draw_left_factor(jax.random.fold_in(seeds[4], 71), 0)
    solved_prev = gaussian(seeds[2], (PREV, VOX), 0.1, 0.59765625, ((0, 32), (1, 16)))
    right_block = gaussian(seeds[3], (PANEL, VOX), 1.0, 6.0, ((0, 32), (1, 16)), jnp.float32)
    return {"gram_panel": gram_panel, "left_factor": left_factor, "solved_prev": solved_prev, "right_block": right_block}


def panel_index():
    grid = jnp.arange(N_ROW, dtype=jnp.int32)[:, None] * ROWS_DEV + jnp.arange(BLOCK, dtype=jnp.int32)[None, :]
    return grid.reshape(-1).astype(jnp.int32)

def reference(gram_panel, left_factor, solved_prev, right_block):
    chosen = left_factor[panel_index()]
    update = gram_panel - jnp.dot(left_factor.astype(jnp.float32), chosen.T.astype(jnp.float32), preferred_element_type=jnp.float32)
    diagonal = update[panel_index()]
    factor = jnp.linalg.cholesky(diagonal)
    inverse = jax.scipy.linalg.solve_triangular(factor, jnp.eye(PANEL, dtype=jnp.float32), lower=True)
    panel_factor = jnp.dot(update, inverse.T, precision=lax.Precision.HIGHEST)
    reduced = right_block - jnp.dot(chosen.astype(jnp.float32), solved_prev.astype(jnp.float32), preferred_element_type=jnp.float32)
    solved_panel = jnp.dot(inverse, reduced, precision=lax.Precision.HIGHEST)
    return (panel_factor, solved_panel)
```

```python
import jax
import jax.numpy as jnp
from jax import lax
from jax.experimental import pallas as pl
from jax.experimental.pallas import tpu as pltpu
from jax.sharding import PartitionSpec as P

HI = lax.Precision.HIGHEST


def factor_block(s_ref):
    lane = lax.broadcasted_iota(jnp.int32, (8, 128), 1)
    sub = lax.broadcasted_iota(jnp.int32, (8, 128), 0)
    for g in range(16):
        base = 8 * g
        inside = (lane >= base) & (lane < base + 8)
        w = s_ref[base:base + 8, :]
        x = [[None] * 8 for _ in range(8)]
        for j in range(8):
            c = jnp.broadcast_to(w[:, base + j:base + j + 1], (8, 128))
            for i in range(j, 8):
                x[i][j] = jnp.broadcast_to(c[i:i + 1, :], (8, 128))
        start = jnp.where(lane == sub + base, 1.0, jnp.where(inside, 0.0, w))
        r = [jnp.broadcast_to(start[j:j + 1, :], (8, 128)) for j in range(8)]
        m = [[None] * 8 for _ in range(8)]
        q = [None] * 8
        top = None
        for j in range(8):
            s = lax.rsqrt(x[j][j])
            t = r[j] * s
            top = t if top is None else jnp.where(sub == j, t, top)
            m[j][j] = s
            for k in range(j):
                m[j][k] = m[j][k] * s
            for k in range(j + 1):
                part = m[j][k] * t
                q[k] = part if q[k] is None else q[k] + part
            col = {i: x[i][j] * s for i in range(j + 1, 8)}
            for i in range(j + 1, 8):
                for k in range(j + 1, i + 1):
                    x[i][k] = x[i][k] - col[i] * col[k]
                r[i] = r[i] - col[i] * t
                for k in range(j + 1):
                    part = col[i] * m[j][k]
                    m[i][k] = -part if m[i][k] is None else m[i][k] - part
        s_ref[base:base + 8, :] = top
        for v in range(g + 1, 16):
            wv = s_ref[8 * v:8 * v + 8, :]
            acc = jnp.where(inside, 0.0, wv)
            for j in range(8):
                acc = acc - jnp.broadcast_to(wv[:, base + j:base + j + 1], (8, 128)) * q[j]
            s_ref[8 * v:8 * v + 8, :] = acc
    rows = lax.broadcasted_iota(jnp.int32, (128, 128), 0)
    cols = lax.broadcasted_iota(jnp.int32, (128, 128), 1)
    s_ref[...] = jnp.where(cols <= rows, s_ref[...], 0.0)


def mm(a, b):
    return lax.dot_general(a, b, (((1,), (0,)), ((), ())), precision=HI, preferred_element_type=jnp.float32)


def mtm(a, b):
    return lax.dot_general(a, b, (((0,), (0,)), ((), ())), precision=HI, preferred_element_type=jnp.float32)


def kernel(a_ref, w_ref, s_ref, m_ref):
    n = a_ref.shape[0]
    big = n // 256
    for j in range(big):
        w_ref[j] = a_ref[:, 256 * j:256 * j + 256]

    def step(b, carry):
        top = pl.multiple_of(b * 256, 256)
        mid = pl.multiple_of(b * 256 + 128, 128)

        def half(h, carry):
            @pl.when(h == 0)
            def _():
                s_ref[...] = w_ref[b, pl.ds(top, 128), 0:128]

            @pl.when(h == 1)
            def _():
                m_ref[0:128, 0:128] = s_ref[...]
                upper = mm(s_ref[...], w_ref[b, pl.ds(top, 128), 128:256])
                m_ref[0:128, 128:256] = upper
                s_ref[...] = w_ref[b, pl.ds(mid, 128), 128:256] - mtm(upper, upper)

            factor_block(s_ref)
            return carry

        lax.fori_loop(0, 2, half, 0)
        lower = mtm(m_ref[0:128, 128:256], m_ref[0:128, 0:128])
        m_ref[128:256, 0:128] = -mm(s_ref[...], lower)
        m_ref[0:128, 128:256] = jnp.zeros((128, 128), jnp.float32)
        m_ref[128:256, 128:256] = s_ref[...]
        inv = m_ref[...]

        for j in range(big):
            w_ref[j, pl.ds(top, 256), :] = mm(inv, w_ref[j, pl.ds(top, 256), :])
        w_ref[b, pl.ds(top, 256), :] = inv

        def below(i, carry):
            at = pl.multiple_of(i * 256, 256)
            w_ref[b, pl.ds(at, 256), :] = jnp.zeros((256, 256), jnp.float32)
            lt = w_ref[i, pl.ds(top, 256), :]
            for j in range(big):
                @pl.when((j <= b) | (j >= i))
                def _():
                    w_ref[j, pl.ds(at, 256), :] = w_ref[j, pl.ds(at, 256), :] - mtm(lt, w_ref[j, pl.ds(top, 256), :])
            w_ref[i, pl.ds(top, 256), :] = jnp.zeros((256, 256), jnp.float32)
            return carry

        lax.fori_loop(b + 1, big, below, 0)
        return carry

    lax.fori_loop(0, big, step, 0)


def invert(diagonal):
    n = diagonal.shape[0]
    return pl.pallas_call(
        kernel,
        out_shape=jax.ShapeDtypeStruct((n // 256, n, 256), jnp.float32),
        in_specs=[pl.BlockSpec(memory_space=pltpu.VMEM)],
        out_specs=pl.BlockSpec(memory_space=pltpu.VMEM),
        scratch_shapes=[pltpu.VMEM((128, 128), jnp.float32), pltpu.VMEM((256, 256), jnp.float32)],
        compiler_params=pltpu.CompilerParams(vmem_limit_bytes=32 * 1024 * 1024),
    )(diagonal)


def split_three(value):
    high = lax.reduce_precision(value, 8, 7)
    rest = value - high
    middle = lax.reduce_precision(rest, 8, 7)
    return [part.astype(jnp.bfloat16) for part in (high, middle, rest - middle)]


def collect(value, axis, count, groups=None):
    many = jnp.broadcast_to(value[None], (count,) + value.shape)
    return lax.all_to_all(many, axis, 0, 0, axis_index_groups=groups)


def body(gram_panel, left_factor, solved_prev, right_block):
    row_count = lax.axis_size("row")
    col_count = lax.axis_size("col")
    row_place = lax.axis_index("row")
    col_place = lax.axis_index("col")
    block_rows = right_block.shape[0]
    col_width = gram_panel.shape[1]
    panel = block_rows * row_count
    depth = left_factor.shape[1]
    wide = 4
    tall = row_count // wide
    chips = col_count // 2
    x_place = row_place % wide
    along_x = [[y * wide + x for x in range(wide)] for y in range(tall)]
    along_y = [[y * wide + x for y in range(tall)] for x in range(wide)]
    along_z = [[z * 2 + core for z in range(chips)] for core in range(2)]
    own = left_factor[:block_rows]
    per_col = row_count // col_count
    strip = depth // per_col

    both = ("row", "col")
    pieces = []
    for turn in range(per_col):
        half = (row_place + turn) % per_col
        sent = lax.dynamic_slice_in_dim(own, half * strip, strip, 1)
        pairs = []
        for r in range(row_count):
            for c in range(col_count):
                to_row = per_col * c + (r + turn) % per_col
                pairs.append((r * col_count + c, to_row * col_count + r // per_col))
        pieces.append(lax.ppermute(sent, both, pairs))
    flip = (row_place % per_col) == 1
    mine = jnp.concatenate(
        [jnp.where(flip, pieces[1], pieces[0]), jnp.where(flip, pieces[0], pieces[1])], axis=0
    )
    strip_piece = lax.all_gather(mine, "col", axis=0, tiled=True)

    gram_parts = split_three(gram_panel[:block_rows])
    packed = jnp.concatenate([own] + gram_parts, axis=1)
    from_x = collect(packed, "row", wide, along_x)
    from_y = collect(own, "row", tall, along_y)
    rows_x = from_x[:, :, :depth].reshape(wide * block_rows, depth)
    rows_y = from_y.reshape(tall * block_rows, depth)
    gram_x = from_x[:, :, depth:].astype(jnp.float32).reshape(wide * block_rows, 3, per_col, block_rows)
    gram_x = gram_x[:, 0] + gram_x[:, 1] + gram_x[:, 2]
    per_x = wide // per_col
    gram_own = lax.dynamic_index_in_dim(gram_x, x_place % per_col, 1, keepdims=False)
    has_gram = (col_place % per_x) == (x_place // per_col)
    y_at = lax.broadcasted_iota(jnp.int32, (1, tall, 1), 1)
    placed = jnp.where(has_gram & (y_at == col_place // per_x), gram_own[:, None, :], 0.0)
    partial = placed.reshape(wide * block_rows, tall * block_rows) - lax.dot_general(
        rows_x, rows_y, (((1,), (1,)), ((), ())), preferred_element_type=jnp.float32
    )
    thin = wide * block_rows // col_count
    partial = partial.reshape(col_count, thin, tall * block_rows)
    own_diag = jnp.sum(lax.all_to_all(partial, "col", 0, 0), axis=0)
    diag_z = collect(own_diag, "col", chips, along_z)
    diag_row = collect(diag_z.reshape(chips * thin, tall * block_rows), "row", row_count)
    other = lax.ppermute(diag_row, "col", [(i, i ^ 1) for i in range(col_count)])
    even = (col_place % 2) == 0
    pair = jnp.stack([jnp.where(even, diag_row, other), jnp.where(even, other, diag_row)], axis=0)
    pair = pair.reshape(2, tall, wide, chips, thin, tall, block_rows)
    diagonal = pair.transpose(1, 3, 0, 4, 5, 2, 6).reshape(panel, panel)
    inverse = invert(diagonal)

    chosen = lax.all_gather(rows_y, "row", axis=0, tiled=False, axis_index_groups=along_x)
    chosen = chosen.reshape(wide, tall, block_rows, depth).transpose(1, 0, 2, 3).reshape(panel, depth)
    summed = lax.psum_scatter(
        lax.dot_general(chosen, left_factor, (((1,), (1,)), ((), ())), preferred_element_type=jnp.float32),
        "col",
        scatter_dimension=0,
        tiled=True,
    )
    update = lax.all_gather(gram_panel.T - summed, "col", axis=0, tiled=True)

    product = jnp.dot(strip_piece, solved_prev, preferred_element_type=jnp.float32)
    product = product.reshape(row_count, block_rows, product.shape[1])
    reduced = right_block - jnp.sum(lax.all_to_all(product, "row", 0, 0), axis=0)
    reduced = lax.all_gather(reduced, "row", axis=0, tiled=True)

    def rows_of_inverse(start, size):
        part = lax.dynamic_slice_in_dim(inverse, start, size, 1)
        return part.transpose(1, 0, 2).reshape(size, panel)

    panel_factor = mm(rows_of_inverse(col_place * col_width, col_width), update).T
    solved_panel = mm(rows_of_inverse(row_place * block_rows, block_rows), reduced)
    return (panel_factor, solved_panel)


def solution(mesh):
    in_specs = (P("row", "col"), P("row", "col"), P("row", "col"), P("row", "col"))
    out_specs = (P("row", "col"), P("row", "col"))
    return jax.shard_map(body, mesh=mesh, in_specs=in_specs, out_specs=out_specs, check_vma=False)
```

```python
import jax
import jax.numpy as jnp
from jax import lax
from jax.experimental import pallas as pl
from jax.experimental.pallas import tpu as pltpu
from jax.sharding import PartitionSpec as P

HI = lax.Precision.HIGHEST


def factor_block(s_ref):
    lane = lax.broadcasted_iota(jnp.int32, (8, 128), 1)
    sub = lax.broadcasted_iota(jnp.int32, (8, 128), 0)
    for g in range(16):
        base = 8 * g
        inside = (lane >= base) & (lane < base + 8)
        w = s_ref[base:base + 8, :]
        x = [[None] * 8 for _ in range(8)]
        for j in range(8):
            c = jnp.broadcast_to(w[:, base + j:base + j + 1], (8, 128))
            for i in range(j, 8):
                x[i][j] = jnp.broadcast_to(c[i:i + 1, :], (8, 128))
        start = jnp.where(lane == sub + base, 1.0, jnp.where(inside, 0.0, w))
        r = [jnp.broadcast_to(start[j:j + 1, :], (8, 128)) for j in range(8)]
        m = [[None] * 8 for _ in range(8)]
        q = [None] * 8
        top = None
        for j in range(8):
            s = lax.rsqrt(x[j][j])
            t = r[j] * s
            top = t if top is None else jnp.where(sub == j, t, top)
            m[j][j] = s
            for k in range(j):
                m[j][k] = m[j][k] * s
            for k in range(j + 1):
                part = m[j][k] * t
                q[k] = part if q[k] is None else q[k] + part
            col = {i: x[i][j] * s for i in range(j + 1, 8)}
            for i in range(j + 1, 8):
                for k in range(j + 1, i + 1):
                    x[i][k] = x[i][k] - col[i] * col[k]
                r[i] = r[i] - col[i] * t
                for k in range(j + 1):
                    part = col[i] * m[j][k]
                    m[i][k] = -part if m[i][k] is None else m[i][k] - part
        s_ref[base:base + 8, :] = top
        for v in range(g + 1, 16):
            wv = s_ref[8 * v:8 * v + 8, :]
            acc = jnp.where(inside, 0.0, wv)
            for j in range(8):
                acc = acc - jnp.broadcast_to(wv[:, base + j:base + j + 1], (8, 128)) * q[j]
            s_ref[8 * v:8 * v + 8, :] = acc
    rows = lax.broadcasted_iota(jnp.int32, (128, 128), 0)
    cols = lax.broadcasted_iota(jnp.int32, (128, 128), 1)
    s_ref[...] = jnp.where(cols <= rows, s_ref[...], 0.0)


def mm(a, b):
    return lax.dot_general(a, b, (((1,), (0,)), ((), ())), precision=HI, preferred_element_type=jnp.float32)


def mtm(a, b):
    return lax.dot_general(a, b, (((0,), (0,)), ((), ())), precision=HI, preferred_element_type=jnp.float32)


def mmt(a, b):
    return lax.dot_general(a, b, (((1,), (1,)), ((), ())), precision=HI, preferred_element_type=jnp.float32)


def factor_kernel(core_ref, mine_ref, other_ref, w_ref, s_ref, m_ref):
    big = w_ref.shape[0]
    rows, tall, half, lanes = mine_ref.shape
    wide = rows // tall
    core = core_ref[0]
    for y in range(tall):
        for z in range(y + 1):
            for x in range(wide):
                at = (wide * z + x) * 2 * half
                cols = slice((y % 2) * lanes, (y % 2) * lanes + lanes)
                w_ref[y // 2, pl.ds(pl.multiple_of(at + core * half, half), half), cols] = mine_ref[wide * y + x, z]
                w_ref[y // 2, pl.ds(pl.multiple_of(at + (1 - core) * half, half), half), cols] = other_ref[wide * y + x, z]

    def step(b, carry):
        top = pl.multiple_of(b * 256, 256)
        mid = pl.multiple_of(b * 256 + 128, 128)

        def half_step(h, carry):
            @pl.when(h == 0)
            def _():
                s_ref[...] = w_ref[b, pl.ds(top, 128), 0:128]

            @pl.when(h == 1)
            def _():
                m_ref[0:128, 0:128] = s_ref[...]
                upper = mm(s_ref[...], w_ref[b, pl.ds(top, 128), 128:256])
                m_ref[0:128, 128:256] = upper
                s_ref[...] = w_ref[b, pl.ds(mid, 128), 128:256] - mtm(upper, upper)

            factor_block(s_ref)
            return carry

        lax.fori_loop(0, 2, half_step, 0)
        lower = mtm(m_ref[0:128, 128:256], m_ref[0:128, 0:128])
        m_ref[128:256, 0:128] = -mm(s_ref[...], lower)
        m_ref[0:128, 128:256] = jnp.zeros((128, 128), jnp.float32)
        m_ref[128:256, 128:256] = s_ref[...]
        w_ref[b, pl.ds(top, 256), :] = m_ref[...]

        for j in range(1, big):
            @pl.when(j > b)
            def _():
                w_ref[j, pl.ds(top, 256), :] = mm(m_ref[...], w_ref[j, pl.ds(top, 256), :])

        def below(i, carry):
            at = pl.multiple_of(i * 256, 256)
            for j in range(1, big):
                @pl.when(j >= i)
                def _():
                    w_ref[j, pl.ds(at, 256), :] = w_ref[j, pl.ds(at, 256), :] - mtm(
                        w_ref[i, pl.ds(top, 256), :], w_ref[j, pl.ds(top, 256), :]
                    )
            return carry

        lax.fori_loop(b + 1, big, below, 0)
        return carry

    lax.fori_loop(0, big, step, 0)


def solve_kernel(w_ref, u_ref, v_ref, out_u_ref, out_v_ref, x_ref):
    big = w_ref.shape[0]
    n = u_ref.shape[0]
    x_ref[0:n, :] = u_ref[...]
    x_ref[n:, :] = v_ref[...]
    for b in range(big):
        span = slice(256 * b, 256 * b + 256)
        y = mmt(x_ref[:, span], w_ref[b, span, :])
        out_u_ref[:, span] = y[0:n, :]
        out_v_ref[:, span] = y[n:, :]
        for j in range(b + 1, big):
            right = slice(256 * j, 256 * j + 256)
            x_ref[:, right] = x_ref[:, right] - mm(y, w_ref[j, span, :])


def factor(core, mine, other, panel):
    vmem = pl.BlockSpec(memory_space=pltpu.VMEM)
    return pl.pallas_call(
        factor_kernel,
        out_shape=jax.ShapeDtypeStruct((panel // 256, panel, 256), jnp.float32),
        in_specs=[pl.BlockSpec(memory_space=pltpu.SMEM), vmem, vmem],
        out_specs=vmem,
        scratch_shapes=[pltpu.VMEM((128, 128), jnp.float32), pltpu.VMEM((256, 256), jnp.float32)],
        compiler_params=pltpu.CompilerParams(vmem_limit_bytes=32 * 1024 * 1024),
        cost_estimate=pl.CostEstimate(flops=50_000_000_000, transcendentals=0, bytes_accessed=8_000_000),
    )(core, mine, other)


def forward(w, u, v):
    vmem = pl.BlockSpec(memory_space=pltpu.VMEM)
    return pl.pallas_call(
        solve_kernel,
        out_shape=[jax.ShapeDtypeStruct(u.shape, jnp.float32), jax.ShapeDtypeStruct(v.shape, jnp.float32)],
        in_specs=[vmem, vmem, vmem],
        out_specs=[vmem, vmem],
        scratch_shapes=[pltpu.VMEM((u.shape[0] + v.shape[0], u.shape[1]), jnp.float32)],
        compiler_params=pltpu.CompilerParams(vmem_limit_bytes=32 * 1024 * 1024),
    )(w, u, v)


def split_three(value):
    high = lax.reduce_precision(value, 8, 7)
    rest = value - high
    middle = lax.reduce_precision(rest, 8, 7)
    return [part.astype(jnp.bfloat16) for part in (high, middle, rest - middle)]


def collect(value, axis, count, groups=None):
    many = jnp.broadcast_to(value[None], (count,) + value.shape)
    return lax.all_to_all(many, axis, 0, 0, axis_index_groups=groups)


def body(gram_panel, left_factor, solved_prev, right_block):
    row_count = lax.axis_size("row")
    col_count = lax.axis_size("col")
    row_place = lax.axis_index("row")
    col_place = lax.axis_index("col")
    block_rows = right_block.shape[0]
    col_width = gram_panel.shape[1]
    panel = block_rows * row_count
    depth = left_factor.shape[1]
    wide = 4
    tall = row_count // wide
    chips = col_count // 2
    x_place = row_place % wide
    along_x = [[y * wide + x for x in range(wide)] for y in range(tall)]
    along_y = [[y * wide + x for y in range(tall)] for x in range(wide)]
    along_z = [[z * 2 + core for z in range(chips)] for core in range(2)]
    own = left_factor[:block_rows]
    per_col = row_count // col_count
    strip = depth // per_col

    both = ("row", "col")
    pieces = []
    for turn in range(per_col):
        half = (row_place + turn) % per_col
        sent = lax.dynamic_slice_in_dim(own, half * strip, strip, 1)
        pairs = []
        for r in range(row_count):
            for c in range(col_count):
                to_row = per_col * c + (r + turn) % per_col
                pairs.append((r * col_count + c, to_row * col_count + r // per_col))
        pieces.append(lax.ppermute(sent, both, pairs))
    flip = (row_place % per_col) == 1
    mine = jnp.concatenate(
        [jnp.where(flip, pieces[1], pieces[0]), jnp.where(flip, pieces[0], pieces[1])], axis=0
    )
    strip_piece = lax.all_gather(mine, "col", axis=0, tiled=True)

    gram_parts = split_three(gram_panel[:block_rows])
    packed = jnp.concatenate([own] + gram_parts, axis=1)
    from_x = collect(packed, "row", wide, along_x)
    from_y = collect(own, "row", tall, along_y)
    rows_x = from_x[:, :, :depth].reshape(wide * block_rows, depth)
    rows_y = from_y.reshape(tall * block_rows, depth)
    gram_x = from_x[:, :, depth:].astype(jnp.float32).reshape(wide * block_rows, 3, per_col, block_rows)
    gram_x = gram_x[:, 0] + gram_x[:, 1] + gram_x[:, 2]
    per_x = wide // per_col
    gram_own = lax.dynamic_index_in_dim(gram_x, x_place % per_col, 1, keepdims=False)
    has_gram = (col_place % per_x) == (x_place // per_col)
    y_at = lax.broadcasted_iota(jnp.int32, (tall, 1, 1), 0)
    placed = jnp.where(has_gram & (y_at == col_place // per_x), gram_own.T[None], 0.0)
    partial = placed.reshape(tall * block_rows, wide * block_rows) - lax.dot_general(
        rows_y, rows_x, (((1,), (1,)), ((), ())), preferred_element_type=jnp.float32
    )
    thin = tall * block_rows // col_count
    partial = partial.reshape(col_count, thin, wide * block_rows)
    own_diag = jnp.sum(lax.all_to_all(partial, "col", 0, 0), axis=0)
    diag_z = collect(own_diag, "col", chips, along_z)
    diag_row = collect(diag_z, "row", row_count)
    other = lax.ppermute(diag_row, "col", [(i, i ^ 1) for i in range(col_count)])

    chosen = lax.all_gather(rows_y, "row", axis=0, tiled=False, axis_index_groups=along_x)
    chosen = chosen.reshape(wide, tall, block_rows, depth).transpose(1, 0, 2, 3).reshape(panel, depth)
    lane = lax.broadcasted_iota(jnp.int32, (1, panel), 1)
    gram_placed = jnp.where(lane // col_width == col_place, jnp.tile(gram_panel, (1, col_count)), 0.0)
    update = lax.psum_scatter(
        gram_placed
        - lax.dot_general(left_factor, chosen, (((1,), (1,)), ((), ())), preferred_element_type=jnp.float32),
        "col",
        scatter_dimension=0,
        tiled=True,
    )

    right_placed = jnp.where(lane // block_rows == row_place, jnp.tile(right_block.T, (1, row_count)), 0.0)
    product = right_placed - lax.dot_general(
        solved_prev, strip_piece, (((0,), (1,)), ((), ())), preferred_element_type=jnp.float32
    )
    product = product.reshape(row_count, product.shape[0] // row_count, panel)
    reduced = jnp.sum(lax.all_to_all(product, "row", 0, 0), axis=0)

    factored = factor((col_place % 2).reshape(1), diag_row, other, panel)
    rows_out, vox_out = forward(factored, update, reduced)
    rows_out = rows_out.reshape(-1, col_count, col_width).transpose(1, 0, 2)
    panel_factor = lax.all_to_all(rows_out, "col", 0, 0).reshape(-1, col_width)
    vox_out = vox_out.reshape(-1, row_count, block_rows).transpose(1, 0, 2)
    solved_panel = lax.all_to_all(vox_out, "row", 0, 0).reshape(-1, block_rows).T
    return (panel_factor, solved_panel)


def solution(mesh):
    in_specs = (P("row", "col"), P("row", "col"), P("row", "col"), P("row", "col"))
    out_specs = (P("row", "col"), P("row", "col"))
    return jax.shard_map(body, mesh=mesh, in_specs=in_specs, out_specs=out_specs, check_vma=False)
```

```python
import jax
import jax.numpy as jnp
from jax import lax
from jax.experimental import pallas as pl
from jax.experimental.pallas import tpu as pltpu
from jax.sharding import PartitionSpec as P

HI = lax.Precision.HIGHEST


def factor_block(s_ref):
    lane = lax.broadcasted_iota(jnp.int32, (8, 128), 1)
    sub = lax.broadcasted_iota(jnp.int32, (8, 128), 0)
    for g in range(16):
        base = 8 * g
        inside = (lane >= base) & (lane < base + 8)
        w = s_ref[base:base + 8, :]
        x = [[None] * 8 for _ in range(8)]
        for j in range(8):
            c = jnp.broadcast_to(w[:, base + j:base + j + 1], (8, 128))
            for i in range(j, 8):
                x[i][j] = jnp.broadcast_to(c[i:i + 1, :], (8, 128))
        start = jnp.where(lane == sub + base, 1.0, jnp.where(inside, 0.0, w))
        r = [jnp.broadcast_to(start[j:j + 1, :], (8, 128)) for j in range(8)]
        m = [[None] * 8 for _ in range(8)]
        q = [None] * 8
        top = None
        for j in range(8):
            s = lax.rsqrt(x[j][j])
            t = r[j] * s
            top = t if top is None else jnp.where(sub == j, t, top)
            m[j][j] = s
            for k in range(j):
                m[j][k] = m[j][k] * s
            for k in range(j + 1):
                part = m[j][k] * t
                q[k] = part if q[k] is None else q[k] + part
            col = {i: x[i][j] * s for i in range(j + 1, 8)}
            for i in range(j + 1, 8):
                for k in range(j + 1, i + 1):
                    x[i][k] = x[i][k] - col[i] * col[k]
                r[i] = r[i] - col[i] * t
                for k in range(j + 1):
                    part = col[i] * m[j][k]
                    m[i][k] = -part if m[i][k] is None else m[i][k] - part
        s_ref[base:base + 8, :] = top
        for v in range(g + 1, 16):
            wv = s_ref[8 * v:8 * v + 8, :]
            acc = jnp.where(inside, 0.0, wv)
            for j in range(8):
                acc = acc - jnp.broadcast_to(wv[:, base + j:base + j + 1], (8, 128)) * q[j]
            s_ref[8 * v:8 * v + 8, :] = acc
    rows = lax.broadcasted_iota(jnp.int32, (128, 128), 0)
    cols = lax.broadcasted_iota(jnp.int32, (128, 128), 1)
    s_ref[...] = jnp.where(cols <= rows, s_ref[...], 0.0)


def mm(a, b):
    return lax.dot_general(a, b, (((1,), (0,)), ((), ())), precision=HI, preferred_element_type=jnp.float32)


def mtm(a, b):
    return lax.dot_general(a, b, (((0,), (0,)), ((), ())), precision=HI, preferred_element_type=jnp.float32)


def mmt(a, b):
    return lax.dot_general(a, b, (((1,), (1,)), ((), ())), precision=HI, preferred_element_type=jnp.float32)


def factor_kernel(core_ref, mine_ref, other_ref, w_ref, s_ref, m_ref):
    big = w_ref.shape[0]
    rows, tall, half, lanes = mine_ref.shape
    wide = rows // tall
    core = core_ref[0]
    for y in range(tall):
        for z in range(y + 1):
            for x in range(wide):
                at = (wide * z + x) * 2 * half
                cols = slice((y % 2) * lanes, (y % 2) * lanes + lanes)
                w_ref[y // 2, pl.ds(pl.multiple_of(at + core * half, half), half), cols] = mine_ref[wide * y + x, z]
                w_ref[y // 2, pl.ds(pl.multiple_of(at + (1 - core) * half, half), half), cols] = other_ref[wide * y + x, z]

    def step(b, carry):
        top = pl.multiple_of(b * 256, 256)
        mid = pl.multiple_of(b * 256 + 128, 128)

        def half_step(h, carry):
            @pl.when(h == 0)
            def _():
                s_ref[...] = w_ref[b, pl.ds(top, 128), 0:128]

            @pl.when(h == 1)
            def _():
                m_ref[0:128, 0:128] = s_ref[...]
                upper = mm(s_ref[...], w_ref[b, pl.ds(top, 128), 128:256])
                m_ref[0:128, 128:256] = upper
                s_ref[...] = w_ref[b, pl.ds(mid, 128), 128:256] - mtm(upper, upper)

            factor_block(s_ref)
            return carry

        lax.fori_loop(0, 2, half_step, 0)
        lower = mtm(m_ref[0:128, 128:256], m_ref[0:128, 0:128])
        m_ref[128:256, 0:128] = -mm(s_ref[...], lower)
        m_ref[0:128, 128:256] = jnp.zeros((128, 128), jnp.float32)
        m_ref[128:256, 128:256] = s_ref[...]
        w_ref[b, pl.ds(top, 256), :] = m_ref[...]

        for j in range(1, big):
            @pl.when(j > b)
            def _():
                w_ref[j, pl.ds(top, 256), :] = mm(m_ref[...], w_ref[j, pl.ds(top, 256), :])

        def below(i, carry):
            at = pl.multiple_of(i * 256, 256)
            for j in range(1, big):
                @pl.when(j >= i)
                def _():
                    w_ref[j, pl.ds(at, 256), :] = w_ref[j, pl.ds(at, 256), :] - mtm(
                        w_ref[i, pl.ds(top, 256), :], w_ref[j, pl.ds(top, 256), :]
                    )
            return carry

        lax.fori_loop(b + 1, big, below, 0)
        return carry

    lax.fori_loop(0, big, step, 0)


def solve_kernel(w_ref, u_ref, v_ref, out_u_ref, out_v_ref, x_ref):
    big = w_ref.shape[0]
    n = u_ref.shape[0]
    x_ref[0:n, :] = u_ref[...]
    x_ref[n:, :] = v_ref[...]
    for b in range(big):
        span = slice(256 * b, 256 * b + 256)
        y = mmt(x_ref[:, span], w_ref[b, span, :])
        out_u_ref[:, span] = y[0:n, :]
        out_v_ref[:, span] = y[n:, :]
        for j in range(b + 1, big):
            right = slice(256 * j, 256 * j + 256)
            x_ref[:, right] = x_ref[:, right] - mm(y, w_ref[j, span, :])


def factor(core, mine, other, panel):
    vmem = pl.BlockSpec(memory_space=pltpu.VMEM)
    return pl.pallas_call(
        factor_kernel,
        out_shape=jax.ShapeDtypeStruct((panel // 256, panel, 256), jnp.float32),
        in_specs=[pl.BlockSpec(memory_space=pltpu.SMEM), vmem, vmem],
        out_specs=vmem,
        scratch_shapes=[pltpu.VMEM((128, 128), jnp.float32), pltpu.VMEM((256, 256), jnp.float32)],
        compiler_params=pltpu.CompilerParams(vmem_limit_bytes=12 * 1024 * 1024),
        cost_estimate=pl.CostEstimate(flops=50_000_000_000, transcendentals=0, bytes_accessed=8_000_000),
    )(core, mine, other)


def forward(w, u, v):
    vmem = pl.BlockSpec(memory_space=pltpu.VMEM)
    return pl.pallas_call(
        solve_kernel,
        out_shape=[jax.ShapeDtypeStruct(u.shape, jnp.float32), jax.ShapeDtypeStruct(v.shape, jnp.float32)],
        in_specs=[vmem, vmem, vmem],
        out_specs=[vmem, vmem],
        scratch_shapes=[pltpu.VMEM((u.shape[0] + v.shape[0], u.shape[1]), jnp.float32)],
        compiler_params=pltpu.CompilerParams(vmem_limit_bytes=12 * 1024 * 1024),
    )(w, u, v)


def split_three(value):
    high = lax.reduce_precision(value, 8, 7)
    rest = value - high
    middle = lax.reduce_precision(rest, 8, 7)
    return [part.astype(jnp.bfloat16) for part in (high, middle, rest - middle)]


def collect(value, axis, count, groups=None):
    many = jnp.broadcast_to(value[None], (count,) + value.shape)
    return lax.all_to_all(many, axis, 0, 0, axis_index_groups=groups)


def body(gram_panel, left_factor, solved_prev, right_block):
    row_count = lax.axis_size("row")
    col_count = lax.axis_size("col")
    row_place = lax.axis_index("row")
    col_place = lax.axis_index("col")
    block_rows = right_block.shape[0]
    col_width = gram_panel.shape[1]
    panel = block_rows * row_count
    depth = left_factor.shape[1]
    wide = 4
    tall = row_count // wide
    chips = col_count // 2
    x_place = row_place % wide
    along_x = [[y * wide + x for x in range(wide)] for y in range(tall)]
    along_y = [[y * wide + x for y in range(tall)] for x in range(wide)]
    along_z = [[z * 2 + core for z in range(chips)] for core in range(2)]
    own = left_factor[:block_rows]
    per_col = row_count // col_count
    strip = depth // per_col

    both = ("row", "col")
    pieces = []
    for turn in range(per_col):
        half = (row_place + turn) % per_col
        sent = lax.dynamic_slice_in_dim(own, half * strip, strip, 1)
        pairs = []
        for r in range(row_count):
            for c in range(col_count):
                to_row = per_col * c + (r + turn) % per_col
                pairs.append((r * col_count + c, to_row * col_count + r // per_col))
        pieces.append(lax.ppermute(sent, both, pairs))
    flip = (row_place % per_col) == 1
    mine = jnp.concatenate(
        [jnp.where(flip, pieces[1], pieces[0]), jnp.where(flip, pieces[0], pieces[1])], axis=0
    )
    strip_piece = lax.all_gather(mine, "col", axis=0, tiled=True)
    own_late, _ = lax.optimization_barrier((own, mine))

    gram_parts = split_three(gram_panel[:block_rows])
    packed = jnp.concatenate([own] + gram_parts, axis=1)
    from_x = collect(packed, "row", wide, along_x)
    from_y = collect(own_late, "row", tall, along_y)
    rows_x = from_x[:, :, :depth].reshape(wide * block_rows, depth)
    rows_y = from_y.reshape(tall * block_rows, depth)
    gram_x = from_x[:, :, depth:].astype(jnp.float32).reshape(wide * block_rows, 3, per_col, block_rows)
    gram_x = gram_x[:, 0] + gram_x[:, 1] + gram_x[:, 2]
    per_x = wide // per_col
    gram_own = lax.dynamic_index_in_dim(gram_x, x_place % per_col, 1, keepdims=False)
    has_gram = (col_place % per_x) == (x_place // per_col)
    y_at = lax.broadcasted_iota(jnp.int32, (tall, 1, 1), 0)
    placed = jnp.where(has_gram & (y_at == col_place // per_x), gram_own.T[None], 0.0)
    partial = placed.reshape(tall * block_rows, wide * block_rows) - lax.dot_general(
        rows_y, rows_x, (((1,), (1,)), ((), ())), preferred_element_type=jnp.float32
    )
    thin = tall * block_rows // col_count
    partial = partial.reshape(col_count, thin, wide * block_rows)
    lane = lax.broadcasted_iota(jnp.int32, (1, panel), 1)
    right_placed = jnp.where(lane // block_rows == row_place, jnp.tile(right_block.T, (1, row_count)), 0.0)
    product = right_placed - lax.dot_general(
        solved_prev, strip_piece, (((0,), (1,)), ((), ())), preferred_element_type=jnp.float32
    )
    product = product.reshape(row_count, product.shape[0] // row_count, panel)

    own_diag = jnp.sum(lax.all_to_all(partial, "col", 0, 0), axis=0)
    diag_z = collect(own_diag, "col", chips, along_z)
    diag_z, product = lax.optimization_barrier((diag_z, product))
    diag_row = collect(diag_z, "row", row_count)
    other = lax.ppermute(diag_row, "col", [(i, i ^ 1) for i in range(col_count)])

    chosen = lax.all_gather(rows_y, "row", axis=0, tiled=False, axis_index_groups=along_x)
    chosen = chosen.reshape(wide, tall, block_rows, depth).transpose(1, 0, 2, 3).reshape(panel, depth)
    gram_placed = jnp.where(lane // col_width == col_place, jnp.tile(gram_panel, (1, col_count)), 0.0)
    update_part = gram_placed - lax.dot_general(
        left_factor, chosen, (((1,), (1,)), ((), ())), preferred_element_type=jnp.float32
    )
    update = lax.psum_scatter(update_part, "col", scatter_dimension=0, tiled=True)

    product, _ = lax.optimization_barrier((product, diag_row))
    spread_out = lax.all_to_all(product, "row", 0, 0)

    diag_row, other, _, _ = lax.optimization_barrier((diag_row, other, update_part, product))
    factored = factor((col_place % 2).reshape(1), diag_row, other, panel)
    factored, spread_out, update = lax.optimization_barrier((factored, spread_out, update))
    reduced = jnp.sum(spread_out, axis=0)
    rows_out, vox_out = forward(factored, update, reduced)
    rows_out = rows_out.reshape(-1, col_count, col_width).transpose(1, 0, 2)
    panel_factor = lax.all_to_all(rows_out, "col", 0, 0).reshape(-1, col_width)
    vox_out = vox_out.reshape(-1, row_count, block_rows).transpose(1, 0, 2)
    solved_panel = lax.all_to_all(vox_out, "row", 0, 0).reshape(-1, block_rows).T
    return (panel_factor, solved_panel)


def solution(mesh):
    in_specs = (P("row", "col"), P("row", "col"), P("row", "col"), P("row", "col"))
    out_specs = (P("row", "col"), P("row", "col"))
    return jax.shard_map(body, mesh=mesh, in_specs=in_specs, out_specs=out_specs, check_vma=False)
```

```python
import jax
import jax.numpy as jnp
from jax import lax
from jax.experimental import pallas as pl
from jax.experimental.pallas import tpu as pltpu
from jax.sharding import PartitionSpec as P

HI = lax.Precision.HIGHEST


def factor_block(s_ref):
    lane = lax.broadcasted_iota(jnp.int32, (8, 128), 1)
    sub = lax.broadcasted_iota(jnp.int32, (8, 128), 0)
    for g in range(16):
        base = 8 * g
        inside = (lane >= base) & (lane < base + 8)
        w = s_ref[base:base + 8, :]
        x = [[None] * 8 for _ in range(8)]
        for j in range(8):
            c = jnp.broadcast_to(w[:, base + j:base + j + 1], (8, 128))
            for i in range(j, 8):
                x[i][j] = jnp.broadcast_to(c[i:i + 1, :], (8, 128))
        start = jnp.where(lane == sub + base, 1.0, jnp.where(inside, 0.0, w))
        r = [jnp.broadcast_to(start[j:j + 1, :], (8, 128)) for j in range(8)]
        m = [[None] * 8 for _ in range(8)]
        q = [None] * 8
        top = None
        for j in range(8):
            s = lax.rsqrt(x[j][j])
            t = r[j] * s
            top = t if top is None else jnp.where(sub == j, t, top)
            m[j][j] = s
            for k in range(j):
                m[j][k] = m[j][k] * s
            for k in range(j + 1):
                part = m[j][k] * t
                q[k] = part if q[k] is None else q[k] + part
            col = {i: x[i][j] * s for i in range(j + 1, 8)}
            for i in range(j + 1, 8):
                for k in range(j + 1, i + 1):
                    x[i][k] = x[i][k] - col[i] * col[k]
                r[i] = r[i] - col[i] * t
                for k in range(j + 1):
                    part = col[i] * m[j][k]
                    m[i][k] = -part if m[i][k] is None else m[i][k] - part
        s_ref[base:base + 8, :] = top
        for v in range(g + 1, 16):
            wv = s_ref[8 * v:8 * v + 8, :]
            acc = jnp.where(inside, 0.0, wv)
            for j in range(8):
                acc = acc - jnp.broadcast_to(wv[:, base + j:base + j + 1], (8, 128)) * q[j]
            s_ref[8 * v:8 * v + 8, :] = acc
    rows = lax.broadcasted_iota(jnp.int32, (128, 128), 0)
    cols = lax.broadcasted_iota(jnp.int32, (128, 128), 1)
    s_ref[...] = jnp.where(cols <= rows, s_ref[...], 0.0)


def mm(a, b):
    return lax.dot_general(a, b, (((1,), (0,)), ((), ())), precision=HI, preferred_element_type=jnp.float32)


def mtm(a, b):
    return lax.dot_general(a, b, (((0,), (0,)), ((), ())), precision=HI, preferred_element_type=jnp.float32)


def mmt(a, b):
    return lax.dot_general(a, b, (((1,), (1,)), ((), ())), precision=HI, preferred_element_type=jnp.float32)


def factor_kernel(core_ref, mine_ref, other_ref, w_ref, s_ref, m_ref):
    big, n, _ = w_ref.shape
    rows, kept, half, lanes = mine_ref.shape
    tall = n // lanes
    wide = rows // tall
    core = core_ref[0]
    for y in range(tall):
        for d in range(kept):
            z = y - d
            if z < 0 and d * 2 >= tall:
                continue
            for x in range(wide):
                at = (wide * max(z, 0) + x) * 2 * half
                first = pl.ds(pl.multiple_of(at + core * half, half), half)
                second = pl.ds(pl.multiple_of(at + (1 - core) * half, half), half)
                if z >= 0:
                    cols = slice((y % 2) * lanes, (y % 2) * lanes + lanes)
                    w_ref[y // 2, first, cols] = mine_ref[wide * y + x, d]
                    w_ref[y // 2, second, cols] = other_ref[wide * y + x, d]
                else:
                    s_ref[first, :] = mine_ref[wide * y + x, d]
                    s_ref[second, :] = other_ref[wide * y + x, d]
            if z < 0:
                z += tall
                cols = slice((z % 2) * lanes, (z % 2) * lanes + lanes)
                w_ref[z // 2, y * lanes:(y + 1) * lanes, cols] = s_ref[...].T

    def step(b, carry):
        top = pl.multiple_of(b * 256, 256)
        mid = pl.multiple_of(b * 256 + 128, 128)

        def half_step(h, carry):
            @pl.when(h == 0)
            def _():
                s_ref[...] = w_ref[b, pl.ds(top, 128), 0:128]

            @pl.when(h == 1)
            def _():
                m_ref[0:128, 0:128] = s_ref[...]
                upper = mm(s_ref[...], w_ref[b, pl.ds(top, 128), 128:256])
                m_ref[0:128, 128:256] = upper
                s_ref[...] = w_ref[b, pl.ds(mid, 128), 128:256] - mtm(upper, upper)

            factor_block(s_ref)
            return carry

        lax.fori_loop(0, 2, half_step, 0)
        lower = mtm(m_ref[0:128, 128:256], m_ref[0:128, 0:128])
        m_ref[128:256, 0:128] = -mm(s_ref[...], lower)
        m_ref[0:128, 128:256] = jnp.zeros((128, 128), jnp.float32)
        m_ref[128:256, 128:256] = s_ref[...]
        w_ref[b, pl.ds(top, 256), :] = m_ref[...]

        for j in range(1, big):
            @pl.when(j > b)
            def _():
                w_ref[j, pl.ds(top, 256), :] = mm(m_ref[...], w_ref[j, pl.ds(top, 256), :])

        def below(i, carry):
            at = pl.multiple_of(i * 256, 256)
            for j in range(1, big):
                @pl.when(j >= i)
                def _():
                    w_ref[j, pl.ds(at, 256), :] = w_ref[j, pl.ds(at, 256), :] - mtm(
                        w_ref[i, pl.ds(top, 256), :], w_ref[j, pl.ds(top, 256), :]
                    )
            return carry

        lax.fori_loop(b + 1, big, below, 0)
        return carry

    lax.fori_loop(0, big, step, 0)


def solve_kernel(w_ref, u_ref, v_ref, out_u_ref, out_v_ref, x_ref):
    big = w_ref.shape[0]
    n = u_ref.shape[0]
    x_ref[0:n, :] = u_ref[...]
    x_ref[n:, :] = v_ref[...]
    for b in range(big):
        span = slice(256 * b, 256 * b + 256)
        y = mmt(x_ref[:, span], w_ref[b, span, :])
        out_u_ref[:, span] = y[0:n, :]
        out_v_ref[:, span] = y[n:, :]
        for j in range(b + 1, big):
            right = slice(256 * j, 256 * j + 256)
            x_ref[:, right] = x_ref[:, right] - mm(y, w_ref[j, span, :])


def factor(core, mine, other, panel):
    vmem = pl.BlockSpec(memory_space=pltpu.VMEM)
    return pl.pallas_call(
        factor_kernel,
        out_shape=jax.ShapeDtypeStruct((panel // 256, panel, 256), jnp.float32),
        in_specs=[pl.BlockSpec(memory_space=pltpu.SMEM), vmem, vmem],
        out_specs=vmem,
        scratch_shapes=[pltpu.VMEM((128, 128), jnp.float32), pltpu.VMEM((256, 256), jnp.float32)],
        compiler_params=pltpu.CompilerParams(vmem_limit_bytes=12 * 1024 * 1024),
        cost_estimate=pl.CostEstimate(flops=50_000_000_000, transcendentals=0, bytes_accessed=8_000_000),
    )(core, mine, other)


def forward(w, u, v):
    vmem = pl.BlockSpec(memory_space=pltpu.VMEM)
    return pl.pallas_call(
        solve_kernel,
        out_shape=[jax.ShapeDtypeStruct(u.shape, jnp.float32), jax.ShapeDtypeStruct(v.shape, jnp.float32)],
        in_specs=[vmem, vmem, vmem],
        out_specs=[vmem, vmem],
        scratch_shapes=[pltpu.VMEM((u.shape[0] + v.shape[0], u.shape[1]), jnp.float32)],
        compiler_params=pltpu.CompilerParams(vmem_limit_bytes=12 * 1024 * 1024),
    )(w, u, v)


def split_three(value):
    high = lax.reduce_precision(value, 8, 7)
    rest = value - high
    middle = lax.reduce_precision(rest, 8, 7)
    return [part.astype(jnp.bfloat16) for part in (high, middle, rest - middle)]


def collect(value, axis, count, groups=None):
    many = jnp.broadcast_to(value[None], (count,) + value.shape)
    return lax.all_to_all(many, axis, 0, 0, axis_index_groups=groups)


def body(gram_panel, left_factor, solved_prev, right_block):
    row_count = lax.axis_size("row")
    col_count = lax.axis_size("col")
    row_place = lax.axis_index("row")
    col_place = lax.axis_index("col")
    block_rows = right_block.shape[0]
    col_width = gram_panel.shape[1]
    panel = block_rows * row_count
    depth = left_factor.shape[1]
    wide = 4
    tall = row_count // wide
    chips = col_count // 2
    x_place = row_place % wide
    along_x = [[y * wide + x for x in range(wide)] for y in range(tall)]
    along_y = [[y * wide + x for y in range(tall)] for x in range(wide)]
    along_z = [[z * 2 + core for z in range(chips)] for core in range(2)]
    own = left_factor[:block_rows]
    per_col = row_count // col_count
    strip = depth // per_col

    both = ("row", "col")
    pieces = []
    for turn in range(per_col):
        half = (row_place + turn) % per_col
        sent = lax.dynamic_slice_in_dim(own, half * strip, strip, 1)
        pairs = []
        for r in range(row_count):
            for c in range(col_count):
                to_row = per_col * c + (r + turn) % per_col
                pairs.append((r * col_count + c, to_row * col_count + r // per_col))
        pieces.append(lax.ppermute(sent, both, pairs))
    flip = (row_place % per_col) == 1
    mine = jnp.concatenate(
        [jnp.where(flip, pieces[1], pieces[0]), jnp.where(flip, pieces[0], pieces[1])], axis=0
    )
    strip_piece = lax.all_gather(mine, "col", axis=0, tiled=True)
    own_late, _ = lax.optimization_barrier((own, mine))

    gram_parts = split_three(gram_panel[:block_rows])
    packed = jnp.concatenate([own] + gram_parts, axis=1)
    from_x = collect(packed, "row", wide, along_x)
    from_y = collect(own_late, "row", tall, along_y)
    rows_x = from_x[:, :, :depth].reshape(wide * block_rows, depth)
    rows_y = from_y.reshape(tall * block_rows, depth)
    gram_x = from_x[:, :, depth:].astype(jnp.float32).reshape(wide * block_rows, 3, per_col, block_rows)
    gram_x = gram_x[:, 0] + gram_x[:, 1] + gram_x[:, 2]
    per_x = wide // per_col
    gram_own = lax.dynamic_index_in_dim(gram_x, x_place % per_col, 1, keepdims=False)
    has_gram = (col_place % per_x) == (x_place // per_col)
    y_at = lax.broadcasted_iota(jnp.int32, (tall, 1, 1), 0)
    placed = jnp.where(has_gram & (y_at == col_place // per_x), gram_own.T[None], 0.0)
    partial = placed.reshape(tall * block_rows, wide * block_rows) - lax.dot_general(
        rows_y, rows_x, (((1,), (1,)), ((), ())), preferred_element_type=jnp.float32
    )
    kept = tall // 2 + 1
    turned = partial.reshape(tall, block_rows, wide * block_rows)[::-1]
    turned = lax.dynamic_slice_in_dim(jnp.concatenate([turned, turned], axis=0), tall - 1 - row_place // wide, tall, 0)
    thin = tall * block_rows // col_count
    partial = turned.reshape(col_count, thin, wide * block_rows)
    lane = lax.broadcasted_iota(jnp.int32, (1, panel), 1)
    right_placed = jnp.where(lane // block_rows == row_place, jnp.tile(right_block.T, (1, row_count)), 0.0)
    product = right_placed - lax.dot_general(
        solved_prev, strip_piece, (((0,), (1,)), ((), ())), preferred_element_type=jnp.float32
    )
    product = product.reshape(row_count, product.shape[0] // row_count, panel)

    chosen = lax.all_gather(own, "row", axis=0, tiled=True)
    gram_placed = jnp.where(lane // col_width == col_place, jnp.tile(gram_panel, (1, col_count)), 0.0)
    update_part = gram_placed - lax.dot_general(
        left_factor, chosen, (((1,), (1,)), ((), ())), preferred_element_type=jnp.float32
    )

    own_diag = jnp.sum(lax.all_to_all(partial, "col", 0, 0), axis=0)
    diag_z = collect(own_diag, "col", chips, along_z)
    diag_z, product, update_part = lax.optimization_barrier((diag_z[:kept], product, update_part))
    diag_row = collect(diag_z, "row", row_count)
    other = lax.ppermute(diag_row, "col", [(i, i ^ 1) for i in range(col_count)])

    update = lax.psum_scatter(update_part, "col", scatter_dimension=0, tiled=True)

    product, _ = lax.optimization_barrier((product, diag_row))
    spread_out = lax.all_to_all(product, "row", 0, 0)

    diag_row, other, _, _ = lax.optimization_barrier((diag_row, other, update_part, product))
    factored = factor((col_place % 2).reshape(1), diag_row, other, panel)
    factored, spread_out, update = lax.optimization_barrier((factored, spread_out, update))
    reduced = jnp.sum(spread_out, axis=0)
    rows_out, vox_out = forward(factored, update, reduced)
    rows_out = rows_out.reshape(-1, col_count, col_width).transpose(1, 0, 2)
    panel_factor = lax.all_to_all(rows_out, "col", 0, 0).reshape(-1, col_width)
    vox_out = vox_out.reshape(-1, row_count, block_rows).transpose(1, 0, 2)
    solved_panel = lax.all_to_all(vox_out, "row", 0, 0).reshape(-1, block_rows).T
    return (panel_factor, solved_panel)


def solution(mesh):
    in_specs = (P("row", "col"), P("row", "col"), P("row", "col"), P("row", "col"))
    out_specs = (P("row", "col"), P("row", "col"))
    return jax.shard_map(body, mesh=mesh, in_specs=in_specs, out_specs=out_specs, check_vma=False)
```

```python
import jax
import jax.numpy as jnp
from jax import lax
from jax.experimental import pallas as pl
from jax.experimental.pallas import tpu as pltpu
from jax.sharding import PartitionSpec as P

HI = lax.Precision.HIGHEST


def factor_block(s_ref):
    lane = lax.broadcasted_iota(jnp.int32, (8, 128), 1)
    sub = lax.broadcasted_iota(jnp.int32, (8, 128), 0)
    for g in range(16):
        base = 8 * g
        inside = (lane >= base) & (lane < base + 8)
        w = s_ref[base:base + 8, :]
        x = [[None] * 8 for _ in range(8)]
        for j in range(8):
            c = jnp.broadcast_to(w[:, base + j:base + j + 1], (8, 128))
            for i in range(j, 8):
                x[i][j] = jnp.broadcast_to(c[i:i + 1, :], (8, 128))
        start = jnp.where(lane == sub + base, 1.0, jnp.where(inside, 0.0, w))
        r = [jnp.broadcast_to(start[j:j + 1, :], (8, 128)) for j in range(8)]
        m = [[None] * 8 for _ in range(8)]
        q = [None] * 8
        top = None
        for j in range(8):
            s = lax.rsqrt(x[j][j])
            t = r[j] * s
            top = t if top is None else jnp.where(sub == j, t, top)
            m[j][j] = s
            for k in range(j):
                m[j][k] = m[j][k] * s
            for k in range(j + 1):
                part = m[j][k] * t
                q[k] = part if q[k] is None else q[k] + part
            col = {i: x[i][j] * s for i in range(j + 1, 8)}
            for i in range(j + 1, 8):
                for k in range(j + 1, i + 1):
                    x[i][k] = x[i][k] - col[i] * col[k]
                r[i] = r[i] - col[i] * t
                for k in range(j + 1):
                    part = col[i] * m[j][k]
                    m[i][k] = -part if m[i][k] is None else m[i][k] - part
        s_ref[base:base + 8, :] = top
        for v in range(g + 1, 16):
            wv = s_ref[8 * v:8 * v + 8, :]
            acc = jnp.where(inside, 0.0, wv)
            for j in range(8):
                acc = acc - jnp.broadcast_to(wv[:, base + j:base + j + 1], (8, 128)) * q[j]
            s_ref[8 * v:8 * v + 8, :] = acc
    rows = lax.broadcasted_iota(jnp.int32, (128, 128), 0)
    cols = lax.broadcasted_iota(jnp.int32, (128, 128), 1)
    s_ref[...] = jnp.where(cols <= rows, s_ref[...], 0.0)


def mm(a, b):
    return lax.dot_general(a, b, (((1,), (0,)), ((), ())), precision=HI, preferred_element_type=jnp.float32)


def mtm(a, b):
    return lax.dot_general(a, b, (((0,), (0,)), ((), ())), precision=HI, preferred_element_type=jnp.float32)


def mmt(a, b):
    return lax.dot_general(a, b, (((1,), (1,)), ((), ())), precision=HI, preferred_element_type=jnp.float32)


def factor_kernel(core_ref, mine_ref, other_ref, w_ref, s_ref, m_ref):
    big, n, _ = w_ref.shape
    rows, kept, half, lanes = mine_ref.shape
    tall = n // lanes
    wide = rows // tall
    core = core_ref[0]
    for y in range(tall):
        for d in range(kept):
            z = y - d
            if z < 0 and d * 2 >= tall:
                continue
            for x in range(wide):
                at = (wide * max(z, 0) + x) * 2 * half
                first = pl.ds(pl.multiple_of(at + core * half, half), half)
                second = pl.ds(pl.multiple_of(at + (1 - core) * half, half), half)
                if z >= 0:
                    cols = slice((y % 2) * lanes, (y % 2) * lanes + lanes)
                    w_ref[y // 2, first, cols] = mine_ref[wide * y + x, d]
                    w_ref[y // 2, second, cols] = other_ref[wide * y + x, d]
                else:
                    s_ref[first, :] = mine_ref[wide * y + x, d]
                    s_ref[second, :] = other_ref[wide * y + x, d]
            if z < 0:
                z += tall
                cols = slice((z % 2) * lanes, (z % 2) * lanes + lanes)
                w_ref[z // 2, y * lanes:(y + 1) * lanes, cols] = s_ref[...].T

    def step(b, carry):
        top = pl.multiple_of(b * 256, 256)
        mid = pl.multiple_of(b * 256 + 128, 128)

        def half_step(h, carry):
            @pl.when(h == 0)
            def _():
                s_ref[...] = w_ref[b, pl.ds(top, 128), 0:128]

            @pl.when(h == 1)
            def _():
                m_ref[0:128, 0:128] = s_ref[...]
                upper = mm(s_ref[...], w_ref[b, pl.ds(top, 128), 128:256])
                m_ref[0:128, 128:256] = upper
                s_ref[...] = w_ref[b, pl.ds(mid, 128), 128:256] - mtm(upper, upper)

            factor_block(s_ref)
            return carry

        lax.fori_loop(0, 2, half_step, 0)
        lower = mtm(m_ref[0:128, 128:256], m_ref[0:128, 0:128])
        m_ref[128:256, 0:128] = -mm(s_ref[...], lower)
        m_ref[0:128, 128:256] = jnp.zeros((128, 128), jnp.float32)
        m_ref[128:256, 128:256] = s_ref[...]
        w_ref[b, pl.ds(top, 256), :] = m_ref[...]

        for j in range(1, big):
            @pl.when(j > b)
            def _():
                w_ref[j, pl.ds(top, 256), :] = mm(m_ref[...], w_ref[j, pl.ds(top, 256), :])

        def below(i, carry):
            at = pl.multiple_of(i * 256, 256)
            for j in range(1, big):
                @pl.when(j >= i)
                def _():
                    w_ref[j, pl.ds(at, 256), :] = w_ref[j, pl.ds(at, 256), :] - mtm(
                        w_ref[i, pl.ds(top, 256), :], w_ref[j, pl.ds(top, 256), :]
                    )
            return carry

        lax.fori_loop(b + 1, big, below, 0)
        return carry

    lax.fori_loop(0, big, step, 0)


def solve_kernel(w_ref, u_ref, out_ref, x_ref):
    big = w_ref.shape[0]
    x_ref[...] = u_ref[...]
    for b in range(big):
        span = slice(256 * b, 256 * b + 256)
        y = mmt(x_ref[:, span], w_ref[b, span, :])
        out_ref[:, span] = y
        for j in range(b + 1, big):
            right = slice(256 * j, 256 * j + 256)
            x_ref[:, right] = x_ref[:, right] - mm(y, w_ref[j, span, :])


def factor(core, mine, other, panel):
    vmem = pl.BlockSpec(memory_space=pltpu.VMEM)
    return pl.pallas_call(
        factor_kernel,
        out_shape=jax.ShapeDtypeStruct((panel // 256, panel, 256), jnp.float32),
        in_specs=[pl.BlockSpec(memory_space=pltpu.SMEM), vmem, vmem],
        out_specs=vmem,
        scratch_shapes=[pltpu.VMEM((128, 128), jnp.float32), pltpu.VMEM((256, 256), jnp.float32)],
        compiler_params=pltpu.CompilerParams(vmem_limit_bytes=12 * 1024 * 1024),
        cost_estimate=pl.CostEstimate(flops=50_000_000_000, transcendentals=0, bytes_accessed=8_000_000),
    )(core, mine, other)


def forward(w, u):
    vmem = pl.BlockSpec(memory_space=pltpu.VMEM)
    return pl.pallas_call(
        solve_kernel,
        out_shape=jax.ShapeDtypeStruct(u.shape, jnp.float32),
        in_specs=[vmem, vmem],
        out_specs=vmem,
        scratch_shapes=[pltpu.VMEM(u.shape, jnp.float32)],
        compiler_params=pltpu.CompilerParams(vmem_limit_bytes=12 * 1024 * 1024),
    )(w, u)


def split_three(value):
    high = lax.reduce_precision(value, 8, 7)
    rest = value - high
    middle = lax.reduce_precision(rest, 8, 7)
    return [part.astype(jnp.bfloat16) for part in (high, middle, rest - middle)]


def collect(value, axis, count, groups=None):
    many = jnp.broadcast_to(value[None], (count,) + value.shape)
    return lax.all_to_all(many, axis, 0, 0, axis_index_groups=groups)


def body(gram_panel, left_factor, solved_prev, right_block):
    row_count = lax.axis_size("row")
    col_count = lax.axis_size("col")
    row_place = lax.axis_index("row")
    col_place = lax.axis_index("col")
    block_rows = right_block.shape[0]
    col_width = gram_panel.shape[1]
    panel = block_rows * row_count
    depth = left_factor.shape[1]
    wide = 4
    tall = row_count // wide
    chips = col_count // 2
    x_place = row_place % wide
    along_x = [[y * wide + x for x in range(wide)] for y in range(tall)]
    along_y = [[y * wide + x for y in range(tall)] for x in range(wide)]
    along_z = [[z * 2 + core for z in range(chips)] for core in range(2)]
    own = left_factor[:block_rows]
    per_col = row_count // col_count
    strip = depth // per_col
    lane = lax.broadcasted_iota(jnp.int32, (1, panel), 1)

    packed = jnp.concatenate([own] + split_three(gram_panel[:block_rows]), axis=1)
    near = [packed]
    for shift in range(1, wide):
        pairs = [(y * wide + x, y * wide + (x + shift) % wide) for y in range(tall) for x in range(wide)]
        near.append(lax.ppermute(packed, "row", pairs))
    from_x = jnp.stack([lax.select_n((x_place - x) % wide, *near) for x in range(wide)], axis=0)
    from_y = collect(own, "row", tall, along_y)
    rows_x = from_x[:, :, :depth].reshape(wide * block_rows, depth)
    rows_y = from_y.reshape(tall * block_rows, depth)
    gram_x = from_x[:, :, depth:].astype(jnp.float32).reshape(wide * block_rows, 3, per_col, block_rows)
    gram_x = gram_x[:, 0] + gram_x[:, 1] + gram_x[:, 2]
    per_x = wide // per_col
    gram_own = lax.dynamic_index_in_dim(gram_x, x_place % per_col, 1, keepdims=False)
    has_gram = (col_place % per_x) == (x_place // per_col)
    y_at = lax.broadcasted_iota(jnp.int32, (tall, 1, 1), 0)
    placed = jnp.where(has_gram & (y_at == col_place // per_x), gram_own.T[None], 0.0)
    partial = placed.reshape(tall * block_rows, wide * block_rows) - lax.dot_general(
        rows_y, rows_x, (((1,), (1,)), ((), ())), preferred_element_type=jnp.float32
    )
    kept = tall // 2 + 1
    turned = partial.reshape(tall, block_rows, wide * block_rows)[::-1]
    turned = lax.dynamic_slice_in_dim(jnp.concatenate([turned, turned], axis=0), tall - 1 - row_place // wide, tall, 0)
    thin = tall * block_rows // col_count
    partial = turned.reshape(col_count, thin, wide * block_rows)
    own_diag = jnp.sum(lax.all_to_all(partial, "col", 0, 0), axis=0)
    diag_z = collect(own_diag, "col", chips, along_z)

    pieces = []
    for turn in range(per_col):
        half = (row_place + turn) % per_col
        sent = lax.dynamic_slice_in_dim(own, half * strip, strip, 1)
        pairs = []
        for r in range(row_count):
            for c in range(col_count):
                to_row = per_col * c + (r + turn) % per_col
                pairs.append((r * col_count + c, to_row * col_count + r // per_col))
        pieces.append(lax.ppermute(sent, ("row", "col"), pairs))
    flip = (row_place % per_col) == 1
    mine = jnp.concatenate(
        [jnp.where(flip, pieces[1], pieces[0]), jnp.where(flip, pieces[0], pieces[1])], axis=0
    )

    chosen = lax.all_gather(rows_y, "row", axis=0, tiled=False, axis_index_groups=along_x)
    chosen, mine = lax.optimization_barrier((chosen, mine))
    chosen = chosen.reshape(wide, tall, block_rows, depth).transpose(1, 0, 2, 3).reshape(panel, depth)
    gram_placed = jnp.where(lane // col_width == col_place, jnp.tile(gram_panel, (1, col_count)), 0.0)
    update_part = gram_placed - lax.dot_general(
        left_factor, chosen, (((1,), (1,)), ((), ())), preferred_element_type=jnp.float32
    )
    right_placed = jnp.where(lane // block_rows == row_place, jnp.tile(right_block.T, (1, row_count)), 0.0)

    diag_z, update_part, right_placed = lax.optimization_barrier((diag_z[:kept], update_part, right_placed))
    diag_row = collect(diag_z, "row", row_count)
    other = lax.ppermute(diag_row, "col", [(i, i ^ 1) for i in range(col_count)])
    update = lax.psum_scatter(update_part, "col", scatter_dimension=0, tiled=True)

    strip_piece = lax.all_gather(mine, "col", axis=0, tiled=True)
    product = right_placed - lax.dot_general(
        solved_prev, strip_piece, (((0,), (1,)), ((), ())), preferred_element_type=jnp.float32
    )
    product = product.reshape(row_count, product.shape[0] // row_count, panel)
    product, _ = lax.optimization_barrier((product, diag_row))
    spread_out = lax.all_to_all(product, "row", 0, 0)

    diag_row, other, _, _ = lax.optimization_barrier((diag_row, other, update_part, product))
    factored = factor((col_place % 2).reshape(1), diag_row, other, panel)
    factored, spread_out = lax.optimization_barrier((factored, spread_out))
    vox_out = forward(factored, jnp.sum(spread_out, axis=0))
    update, vox_out = lax.optimization_barrier((update, vox_out))
    rows_out = forward(factored, update)
    vox_out = vox_out.reshape(-1, row_count, block_rows).transpose(1, 0, 2)
    solved_panel = lax.all_to_all(vox_out, "row", 0, 0).reshape(-1, block_rows).T
    rows_out, solved_panel = lax.optimization_barrier((rows_out, solved_panel))
    rows_out = rows_out.reshape(-1, col_count, col_width).transpose(1, 0, 2)
    panel_factor = lax.all_to_all(rows_out, "col", 0, 0).reshape(-1, col_width)
    return (panel_factor, solved_panel)


def solution(mesh):
    in_specs = (P("row", "col"), P("row", "col"), P("row", "col"), P("row", "col"))
    out_specs = (P("row", "col"), P("row", "col"))
    return jax.shard_map(body, mesh=mesh, in_specs=in_specs, out_specs=out_specs, check_vma=False)
```

```python
import jax
import jax.numpy as jnp
from jax import lax
from jax.experimental import pallas as pl
from jax.experimental.pallas import tpu as pltpu
from jax.sharding import PartitionSpec as P

HI = lax.Precision.HIGHEST


def factor_block(s_ref, c_ref):
    lane = lax.broadcasted_iota(jnp.int32, (8, 128), 1)
    sub = lax.broadcasted_iota(jnp.int32, (8, 128), 0)

    def wide(value, at):
        return jnp.broadcast_to(value[:, at:at + 1], (8, 128))

    def apply(v, base, q):
        rows = s_ref[8 * v:8 * v + 8, :]
        part = [wide(rows, base + j) * q[j] for j in range(8)]
        total = ((part[0] + part[1]) + (part[2] + part[3])) + ((part[4] + part[5]) + (part[6] + part[7]))
        rows = jnp.where((lane >= base) & (lane < base + 8), 0.0, rows) - total
        s_ref[8 * v:8 * v + 8, :] = rows
        return rows

    w = s_ref[0:8, :]
    follow = s_ref[8:16, :]
    waiting = []
    for g in range(16):
        base = 8 * g
        inside = (lane >= base) & (lane < base + 8)
        x = [[None] * 8 for _ in range(8)]
        for j in range(8):
            c = wide(w, base + j)
            at = 72 * (g % 2) + 8 * j
            c_ref[at:at + 8, :] = c
            for i in range(j, 8):
                x[i][j] = c_ref[pl.ds(at + i, 8, stride=0), :]
        start = jnp.where(lane == sub + base, 1.0, jnp.where(inside, 0.0, w))
        at = 72 * (g % 2) + 64
        c_ref[at:at + 8, :] = start
        r = [c_ref[pl.ds(at + j, 8, stride=0), :] for j in range(8)]
        if g < 15:
            if waiting:
                follow = waiting.pop(0)()
            b = [wide(follow, base + k) for k in range(8)]
            follow = jnp.where(inside, 0.0, follow)
        ahead = [[None] * 8 for _ in range(8)]
        top = None
        share = -(-len(waiting) // 8)
        for j in range(8):
            d = 1.0 / x[j][j]
            s = lax.rsqrt(x[j][j])
            t = r[j] * s
            top = t if top is None else jnp.where(sub == j, t, top)
            f = {i: x[i][j] * d for i in range(j + 1, 8)}
            for i in range(j + 1, 8):
                for k in range(j + 1, i + 1):
                    x[i][k] = x[i][k] - (x[i][j] * x[k][j]) * d if i == j + 1 else x[i][k] - f[i] * x[k][j]
            p = r[j] * d
            for i in range(j + 1, 8):
                r[i] = r[i] - x[i][j] * p
            if g < 15:
                follow = follow - b[j] * p
                for k in range(j + 1, 8):
                    b[k] = b[k] - b[j] * f[k]
            for i in range(j):
                r[i] = r[i] - ahead[i][j] * p
                for k in range(j + 1, 8):
                    ahead[i][k] = ahead[i][k] - ahead[i][j] * f[k]
            r[j] = p
            for k in range(j + 1, 8):
                ahead[j][k] = f[k]
            for _ in range(share):
                if waiting:
                    waiting.pop(0)()
        s_ref[base:base + 8, :] = top
        w = follow
        waiting = [lambda v=v, base=base, q=r: apply(v, base, q) for v in range(g + 2, 16)]
    rows = lax.broadcasted_iota(jnp.int32, (128, 128), 0)
    cols = lax.broadcasted_iota(jnp.int32, (128, 128), 1)
    s_ref[...] = jnp.where(cols <= rows, s_ref[...], 0.0)


def mm(a, b):
    return lax.dot_general(a, b, (((1,), (0,)), ((), ())), precision=HI, preferred_element_type=jnp.float32)


def mtm(a, b):
    return lax.dot_general(a, b, (((0,), (0,)), ((), ())), precision=HI, preferred_element_type=jnp.float32)


def mmt(a, b):
    return lax.dot_general(a, b, (((1,), (1,)), ((), ())), precision=HI, preferred_element_type=jnp.float32)


def factor_kernel(core_ref, mine_ref, other_ref, out_ref, w_ref, s_ref, m_ref, c_ref, sems):
    big, n, _ = w_ref.shape
    rows, kept, half, lanes = mine_ref.shape
    tall = n // lanes
    wide = rows // tall
    core = core_ref[0]
    for y in range(tall):
        for d in range(kept):
            z = y - d
            if z < 0 and d * 2 >= tall:
                continue
            for x in range(wide):
                at = (wide * max(z, 0) + x) * 2 * half
                first = pl.ds(pl.multiple_of(at + core * half, half), half)
                second = pl.ds(pl.multiple_of(at + (1 - core) * half, half), half)
                if z >= 0:
                    cols = slice((y % 2) * lanes, (y % 2) * lanes + lanes)
                    w_ref[y // 2, first, cols] = mine_ref[wide * y + x, d]
                    w_ref[y // 2, second, cols] = other_ref[wide * y + x, d]
                else:
                    s_ref[first, :] = mine_ref[wide * y + x, d]
                    s_ref[second, :] = other_ref[wide * y + x, d]
            if z < 0:
                z += tall
                cols = slice((z % 2) * lanes, (z % 2) * lanes + lanes)
                w_ref[z // 2, y * lanes:(y + 1) * lanes, cols] = s_ref[...].T

    def step(b, carry):
        top = pl.multiple_of(b * 256, 256)
        mid = pl.multiple_of(b * 256 + 128, 128)

        def half_step(h, carry):
            @pl.when(h == 0)
            def _():
                s_ref[...] = w_ref[b, pl.ds(top, 128), 0:128]

            @pl.when(h == 1)
            def _():
                m_ref[0:128, 0:128] = s_ref[...]
                upper = mm(s_ref[...], w_ref[b, pl.ds(top, 128), 128:256])
                m_ref[0:128, 128:256] = upper
                s_ref[...] = w_ref[b, pl.ds(mid, 128), 128:256] - mtm(upper, upper)

            factor_block(s_ref, c_ref)
            return carry

        lax.fori_loop(0, 2, half_step, 0)
        lower = mtm(m_ref[0:128, 128:256], m_ref[0:128, 0:128])
        m_ref[128:256, 0:128] = -mm(s_ref[...], lower)
        m_ref[0:128, 128:256] = jnp.zeros((128, 128), jnp.float32)
        m_ref[128:256, 128:256] = s_ref[...]
        w_ref[b, pl.ds(top, 256), :] = m_ref[...]

        for j in range(1, big):
            @pl.when(j > b)
            def _():
                w_ref[j, pl.ds(top, 256), :] = mm(m_ref[...], w_ref[j, pl.ds(top, 256), :])

        for j in range(big):
            @pl.when(j >= b)
            def _():
                pltpu.make_async_copy(
                    w_ref.at[j, pl.ds(top, 256), :], out_ref.at[j, pl.ds(top, 256), :], sems.at[b, j]
                ).start()

        def below(i, carry):
            at = pl.multiple_of(i * 256, 256)
            for j in range(1, big):
                @pl.when(j >= i)
                def _():
                    w_ref[j, pl.ds(at, 256), :] = w_ref[j, pl.ds(at, 256), :] - mtm(
                        w_ref[i, pl.ds(top, 256), :], w_ref[j, pl.ds(top, 256), :]
                    )
            return carry

        lax.fori_loop(b + 1, big, below, 0)
        return carry

    lax.fori_loop(0, big, step, 0)
    for b in range(big):
        span = pl.ds(256 * b, 256)
        for j in range(b, big):
            pltpu.make_async_copy(w_ref.at[j, span, :], out_ref.at[j, span, :], sems.at[b, j]).wait()


def solve_kernel(from_ref, u_ref, out_ref, w_ref, x_ref, sems):
    big = w_ref.shape[0]
    copies = {}
    for b in range(big):
        span = pl.ds(256 * b, 256)
        for j in range(b, big):
            copies[b, j] = pltpu.make_async_copy(from_ref.at[j, span, :], w_ref.at[j, span, :], sems.at[b, j])
            copies[b, j].start()
    x_ref[...] = u_ref[...]
    for b in range(big):
        span = slice(256 * b, 256 * b + 256)
        copies[b, b].wait()
        y = mmt(x_ref[:, span], w_ref[b, span, :])
        out_ref[:, span] = y
        for j in range(b + 1, big):
            right = slice(256 * j, 256 * j + 256)
            copies[b, j].wait()
            x_ref[:, right] = x_ref[:, right] - mm(y, w_ref[j, span, :])


def factor(core, mine, other, panel):
    vmem = pl.BlockSpec(memory_space=pltpu.VMEM)
    big = panel // 256
    return pl.pallas_call(
        factor_kernel,
        out_shape=pltpu.HBM((big, panel, 256), jnp.float32),
        in_specs=[pl.BlockSpec(memory_space=pltpu.SMEM), vmem, vmem],
        out_specs=pl.BlockSpec(memory_space=pltpu.HBM),
        scratch_shapes=[
            pltpu.VMEM((big, panel, 256), jnp.float32),
            pltpu.VMEM((128, 128), jnp.float32),
            pltpu.VMEM((256, 256), jnp.float32),
            pltpu.VMEM((144, 128), jnp.float32),
            pltpu.SemaphoreType.DMA((big, big)),
        ],
        compiler_params=pltpu.CompilerParams(vmem_limit_bytes=16 * 1024 * 1024),
        cost_estimate=pl.CostEstimate(flops=40_000_000_000, transcendentals=0, bytes_accessed=8_000_000),
    )(core, mine, other)


def forward(w, u):
    vmem = pl.BlockSpec(memory_space=pltpu.VMEM)
    return pl.pallas_call(
        solve_kernel,
        out_shape=jax.ShapeDtypeStruct(u.shape, jnp.float32),
        in_specs=[pl.BlockSpec(memory_space=pltpu.HBM), vmem],
        out_specs=vmem,
        scratch_shapes=[
            pltpu.VMEM(w.shape, jnp.float32),
            pltpu.VMEM(u.shape, jnp.float32),
            pltpu.SemaphoreType.DMA((w.shape[0], w.shape[0])),
        ],
        compiler_params=pltpu.CompilerParams(vmem_limit_bytes=12 * 1024 * 1024),
    )(pltpu.with_memory_space_constraint(w, pltpu.HBM), u)


def split_three(value):
    high = lax.reduce_precision(value, 8, 7)
    rest = value - high
    middle = lax.reduce_precision(rest, 8, 7)
    return [part.astype(jnp.bfloat16) for part in (high, middle, rest - middle)]


def collect(value, axis, count, groups=None):
    many = jnp.broadcast_to(value[None], (count,) + value.shape)
    return lax.all_to_all(many, axis, 0, 0, axis_index_groups=groups)


def body(gram_panel, left_factor, solved_prev, right_block):
    row_count = lax.axis_size("row")
    col_count = lax.axis_size("col")
    row_place = lax.axis_index("row")
    col_place = lax.axis_index("col")
    block_rows = right_block.shape[0]
    col_width = gram_panel.shape[1]
    panel = block_rows * row_count
    depth = left_factor.shape[1]
    wide = 4
    tall = row_count // wide
    chips = col_count // 2
    x_place = row_place % wide
    along_x = [[y * wide + x for x in range(wide)] for y in range(tall)]
    along_y = [[y * wide + x for y in range(tall)] for x in range(wide)]
    along_z = [[z * 2 + core for z in range(chips)] for core in range(2)]
    own = left_factor[:block_rows]
    per_col = row_count // col_count
    strip = depth // per_col
    lane = lax.broadcasted_iota(jnp.int32, (1, panel), 1)

    packed = jnp.concatenate([own] + split_three(gram_panel[:block_rows]), axis=1)
    from_y = collect(own, "row", tall, along_y)
    packed, from_y = lax.optimization_barrier((packed, from_y))
    from_x = collect(packed, "row", wide, along_x)
    rows_x = from_x[:, :, :depth].reshape(wide * block_rows, depth)
    rows_y = from_y.reshape(tall * block_rows, depth)
    gram_x = from_x[:, :, depth:].astype(jnp.float32).reshape(wide * block_rows, 3, per_col, block_rows)
    gram_x = gram_x[:, 0] + gram_x[:, 1] + gram_x[:, 2]
    per_x = wide // per_col
    gram_own = lax.dynamic_index_in_dim(gram_x, x_place % per_col, 1, keepdims=False)
    has_gram = (col_place % per_x) == (x_place // per_col)
    y_at = lax.broadcasted_iota(jnp.int32, (tall, 1, 1), 0)
    placed = jnp.where(has_gram & (y_at == col_place // per_x), gram_own.T[None], 0.0)
    partial = placed.reshape(tall * block_rows, wide * block_rows) - lax.dot_general(
        rows_y, rows_x, (((1,), (1,)), ((), ())), preferred_element_type=jnp.float32
    )
    kept = tall // 2 + 1
    turned = partial.reshape(tall, block_rows, wide * block_rows)[::-1]
    turned = lax.dynamic_slice_in_dim(jnp.concatenate([turned, turned], axis=0), tall - 1 - row_place // wide, tall, 0)
    thin = tall * block_rows // col_count
    partial = turned.reshape(col_count, thin, wide * block_rows)

    own_late, partial_now = lax.optimization_barrier((own, partial))
    own_diag = jnp.sum(lax.all_to_all(partial_now, "col", 0, 0), axis=0)
    diag_z = collect(own_diag, "col", chips, along_z)
    pieces = []
    for turn in range(per_col):
        half = (row_place + turn) % per_col
        sent = lax.dynamic_slice_in_dim(own_late, half * strip, strip, 1)
        pairs = []
        for r in range(row_count):
            for c in range(col_count):
                to_row = per_col * c + (r + turn) % per_col
                pairs.append((r * col_count + c, to_row * col_count + r // per_col))
        pieces.append(lax.ppermute(sent, ("row", "col"), pairs))
    flip = (row_place % per_col) == 1
    mine = jnp.concatenate(
        [jnp.where(flip, pieces[1], pieces[0]), jnp.where(flip, pieces[0], pieces[1])], axis=0
    )

    chosen = lax.all_gather(rows_y, "row", axis=0, tiled=False, axis_index_groups=along_x)
    chosen = chosen.reshape(wide, tall, block_rows, depth).transpose(1, 0, 2, 3).reshape(panel, depth)
    gram_placed = jnp.where(lane // col_width == col_place, jnp.tile(gram_panel, (1, col_count)), 0.0)
    update_part = gram_placed - lax.dot_general(
        left_factor, chosen, (((1,), (1,)), ((), ())), preferred_element_type=jnp.float32
    )
    right_placed = jnp.where(lane // block_rows == row_place, jnp.tile(right_block.T, (1, row_count)), 0.0)

    diag_z, update_part, right_placed, _ = lax.optimization_barrier((diag_z[:kept], update_part, right_placed, mine))
    diag_row = collect(diag_z, "row", row_count)
    other = lax.ppermute(diag_row, "col", [(i, i ^ 1) for i in range(col_count)])
    update = lax.psum_scatter(update_part, "col", scatter_dimension=0, tiled=True)

    strip_piece = lax.all_gather(mine, "col", axis=0, tiled=True)
    product = right_placed - lax.dot_general(
        solved_prev, strip_piece, (((0,), (1,)), ((), ())), preferred_element_type=jnp.float32
    )
    product = product.reshape(row_count, product.shape[0] // row_count, panel)
    product, _ = lax.optimization_barrier((product, diag_row))
    spread_out = lax.all_to_all(product, "row", 0, 0)

    diag_row, other, _, _ = lax.optimization_barrier((diag_row, other, update_part, product))
    factored = factor((col_place % 2).reshape(1), diag_row, other, panel)
    factored, spread_out = lax.optimization_barrier((factored, spread_out))
    vox_out = forward(factored, jnp.sum(spread_out, axis=0))
    update, vox_out = lax.optimization_barrier((update, vox_out))
    rows_out = forward(factored, update)
    vox_out = vox_out.reshape(-1, row_count, block_rows).transpose(1, 0, 2)
    solved_panel = lax.all_to_all(vox_out, "row", 0, 0).reshape(-1, block_rows).T
    rows_out, solved_panel = lax.optimization_barrier((rows_out, solved_panel))
    rows_out = rows_out.reshape(-1, col_count, col_width).transpose(1, 0, 2)
    panel_factor = lax.all_to_all(rows_out, "col", 0, 0).reshape(-1, col_width)
    return (panel_factor, solved_panel)


def solution(mesh):
    in_specs = (P("row", "col"), P("row", "col"), P("row", "col"), P("row", "col"))
    out_specs = (P("row", "col"), P("row", "col"))
    return jax.shard_map(body, mesh=mesh, in_specs=in_specs, out_specs=out_specs, check_vma=False)
```

```python
import jax
import jax.numpy as jnp
from jax import lax
from jax.experimental import pallas as pl
from jax.experimental.pallas import tpu as pltpu
from jax.sharding import PartitionSpec as P

HI = lax.Precision.HIGHEST


def factor_block(s_ref, c_ref):
    lane = lax.broadcasted_iota(jnp.int32, (8, 128), 1)
    sub = lax.broadcasted_iota(jnp.int32, (8, 128), 0)

    def wide(value, at):
        return jnp.broadcast_to(value[:, at:at + 1], (8, 128))

    def apply(v, base, q):
        rows = s_ref[8 * v:8 * v + 8, :]
        part = [wide(rows, base + j) * q[j] for j in range(8)]
        total = ((part[0] + part[1]) + (part[2] + part[3])) + ((part[4] + part[5]) + (part[6] + part[7]))
        rows = jnp.where((lane >= base) & (lane < base + 8), 0.0, rows) - total
        s_ref[8 * v:8 * v + 8, :] = rows
        return rows

    w = s_ref[0:8, :]
    follow = s_ref[8:16, :]
    waiting = []
    for g in range(16):
        base = 8 * g
        inside = (lane >= base) & (lane < base + 8)
        x = [[None] * 8 for _ in range(8)]
        for j in range(8):
            c = wide(w, base + j)
            at = 72 * (g % 2) + 8 * j
            c_ref[at:at + 8, :] = c
            for i in range(j, 8):
                x[i][j] = c_ref[pl.ds(at + i, 8, stride=0), :]
        start = jnp.where(lane == sub + base, 1.0, jnp.where(inside, 0.0, w))
        at = 72 * (g % 2) + 64
        c_ref[at:at + 8, :] = start
        r = [c_ref[pl.ds(at + j, 8, stride=0), :] for j in range(8)]
        if g < 15:
            if waiting:
                follow = waiting.pop(0)()
            b = [wide(follow, base + k) for k in range(8)]
            follow = jnp.where(inside, 0.0, follow)
        ahead = [[None] * 8 for _ in range(8)]
        top = None
        share = -(-len(waiting) // 8)
        for j in range(8):
            d = 1.0 / x[j][j]
            s = lax.rsqrt(x[j][j])
            t = r[j] * s
            top = t if top is None else jnp.where(sub == j, t, top)
            f = {i: x[i][j] * d for i in range(j + 1, 8)}
            for i in range(j + 1, 8):
                for k in range(j + 1, i + 1):
                    x[i][k] = x[i][k] - (x[i][j] * x[k][j]) * d if i == j + 1 else x[i][k] - f[i] * x[k][j]
            p = r[j] * d
            for i in range(j + 1, 8):
                r[i] = r[i] - x[i][j] * p
            if g < 15:
                follow = follow - b[j] * p
                for k in range(j + 1, 8):
                    b[k] = b[k] - b[j] * f[k]
            for i in range(j):
                r[i] = r[i] - ahead[i][j] * p
                for k in range(j + 1, 8):
                    ahead[i][k] = ahead[i][k] - ahead[i][j] * f[k]
            r[j] = p
            for k in range(j + 1, 8):
                ahead[j][k] = f[k]
            for _ in range(share):
                if waiting:
                    waiting.pop(0)()
        s_ref[base:base + 8, :] = top
        w = follow
        waiting = [lambda v=v, base=base, q=r: apply(v, base, q) for v in range(g + 2, 16)]
    rows = lax.broadcasted_iota(jnp.int32, (128, 128), 0)
    cols = lax.broadcasted_iota(jnp.int32, (128, 128), 1)
    s_ref[...] = jnp.where(cols <= rows, s_ref[...], 0.0)


def mm(a, b):
    return lax.dot_general(a, b, (((1,), (0,)), ((), ())), precision=HI, preferred_element_type=jnp.float32)


def mtm(a, b):
    return lax.dot_general(a, b, (((0,), (0,)), ((), ())), precision=HI, preferred_element_type=jnp.float32)


def mmt(a, b):
    return lax.dot_general(a, b, (((1,), (1,)), ((), ())), precision=HI, preferred_element_type=jnp.float32)


def factor_kernel(core_ref, mine_ref, other_ref, out_ref, w_ref, s_ref, m_ref, c_ref, sems):
    big, n, _ = w_ref.shape
    rows, kept, half, lanes = mine_ref.shape
    tall = n // lanes
    wide = rows // tall
    core = core_ref[0]
    for y in range(tall):
        for d in range(kept):
            z = y - d
            if z < 0 and d * 2 >= tall:
                continue
            for x in range(wide):
                at = (wide * max(z, 0) + x) * 2 * half
                first = pl.ds(pl.multiple_of(at + core * half, half), half)
                second = pl.ds(pl.multiple_of(at + (1 - core) * half, half), half)
                if z >= 0:
                    cols = slice((y % 2) * lanes, (y % 2) * lanes + lanes)
                    w_ref[y // 2, first, cols] = mine_ref[wide * y + x, d]
                    w_ref[y // 2, second, cols] = other_ref[wide * y + x, d]
                else:
                    s_ref[first, :] = mine_ref[wide * y + x, d]
                    s_ref[second, :] = other_ref[wide * y + x, d]
            if z < 0:
                z += tall
                cols = slice((z % 2) * lanes, (z % 2) * lanes + lanes)
                w_ref[z // 2, y * lanes:(y + 1) * lanes, cols] = s_ref[...].T

    def step(b, carry):
        top = pl.multiple_of(b * 256, 256)
        mid = pl.multiple_of(b * 256 + 128, 128)

        def half_step(h, carry):
            @pl.when(h == 0)
            def _():
                s_ref[...] = w_ref[b, pl.ds(top, 128), 0:128]

            @pl.when(h == 1)
            def _():
                m_ref[0:128, 0:128] = s_ref[...]
                upper = mm(s_ref[...], w_ref[b, pl.ds(top, 128), 128:256])
                m_ref[0:128, 128:256] = upper
                s_ref[...] = w_ref[b, pl.ds(mid, 128), 128:256] - mtm(upper, upper)

            factor_block(s_ref, c_ref)
            return carry

        lax.fori_loop(0, 2, half_step, 0)
        lower = mtm(m_ref[0:128, 128:256], m_ref[0:128, 0:128])
        m_ref[128:256, 0:128] = -mm(s_ref[...], lower)
        m_ref[0:128, 128:256] = jnp.zeros((128, 128), jnp.float32)
        m_ref[128:256, 128:256] = s_ref[...]
        w_ref[b, pl.ds(top, 256), :] = m_ref[...]

        for j in range(1, big):
            @pl.when(j > b)
            def _():
                w_ref[j, pl.ds(top, 256), :] = mm(m_ref[...], w_ref[j, pl.ds(top, 256), :])

        for j in range(big):
            @pl.when(j >= b)
            def _():
                pltpu.make_async_copy(
                    w_ref.at[j, pl.ds(top, 256), :], out_ref.at[j, pl.ds(top, 256), :], sems.at[b, j]
                ).start()

        def below(i, carry):
            at = pl.multiple_of(i * 256, 256)
            for j in range(1, big):
                @pl.when(j >= i)
                def _():
                    w_ref[j, pl.ds(at, 256), :] = w_ref[j, pl.ds(at, 256), :] - mtm(
                        w_ref[i, pl.ds(top, 256), :], w_ref[j, pl.ds(top, 256), :]
                    )
            return carry

        lax.fori_loop(b + 1, big, below, 0)
        return carry

    lax.fori_loop(0, big, step, 0)
    for b in range(big):
        span = pl.ds(256 * b, 256)
        for j in range(b, big):
            pltpu.make_async_copy(w_ref.at[j, span, :], out_ref.at[j, span, :], sems.at[b, j]).wait()


def solve_kernel(from_ref, u_ref, v_ref, out_u_ref, out_v_ref, w_ref, x_ref, sems):
    big = w_ref.shape[0]
    n = u_ref.shape[0]
    copies = {}
    for b in range(big):
        span = pl.ds(256 * b, 256)
        for j in range(b, big):
            copies[b, j] = pltpu.make_async_copy(from_ref.at[j, span, :], w_ref.at[j, span, :], sems.at[b, j])
            copies[b, j].start()
    x_ref[0:n, :] = u_ref[...]
    x_ref[n:, :] = v_ref[...]
    for b in range(big):
        span = slice(256 * b, 256 * b + 256)
        copies[b, b].wait()
        y = mmt(x_ref[:, span], w_ref[b, span, :])
        out_u_ref[:, span] = y[0:n, :]
        out_v_ref[:, span] = y[n:, :]
        for j in range(b + 1, big):
            right = slice(256 * j, 256 * j + 256)
            copies[b, j].wait()
            x_ref[:, right] = x_ref[:, right] - mm(y, w_ref[j, span, :])


def factor(core, mine, other, panel):
    vmem = pl.BlockSpec(memory_space=pltpu.VMEM)
    big = panel // 256
    return pl.pallas_call(
        factor_kernel,
        out_shape=pltpu.HBM((big, panel, 256), jnp.float32),
        in_specs=[pl.BlockSpec(memory_space=pltpu.SMEM), vmem, vmem],
        out_specs=pl.BlockSpec(memory_space=pltpu.HBM),
        scratch_shapes=[
            pltpu.VMEM((big, panel, 256), jnp.float32),
            pltpu.VMEM((128, 128), jnp.float32),
            pltpu.VMEM((256, 256), jnp.float32),
            pltpu.VMEM((144, 128), jnp.float32),
            pltpu.SemaphoreType.DMA((big, big)),
        ],
        compiler_params=pltpu.CompilerParams(vmem_limit_bytes=16 * 1024 * 1024),
        cost_estimate=pl.CostEstimate(flops=panel**3, transcendentals=0, bytes_accessed=8 * panel * panel),
    )(core, mine, other)


def forward(w, u, v):
    vmem = pl.BlockSpec(memory_space=pltpu.VMEM)
    return pl.pallas_call(
        solve_kernel,
        out_shape=[jax.ShapeDtypeStruct(u.shape, jnp.float32), jax.ShapeDtypeStruct(v.shape, jnp.float32)],
        in_specs=[pl.BlockSpec(memory_space=pltpu.HBM), vmem, vmem],
        out_specs=[vmem, vmem],
        scratch_shapes=[
            pltpu.VMEM(w.shape, jnp.float32),
            pltpu.VMEM((u.shape[0] + v.shape[0], u.shape[1]), jnp.float32),
            pltpu.SemaphoreType.DMA((w.shape[0], w.shape[0])),
        ],
        compiler_params=pltpu.CompilerParams(vmem_limit_bytes=12 * 1024 * 1024),
    )(pltpu.with_memory_space_constraint(w, pltpu.HBM), u, v)


def split_three(value):
    high = lax.reduce_precision(value, 8, 7)
    rest = value - high
    middle = lax.reduce_precision(rest, 8, 7)
    return [part.astype(jnp.bfloat16) for part in (high, middle, rest - middle)]


def collect(value, axis, count, groups=None):
    many = jnp.broadcast_to(value[None], (count,) + value.shape)
    return lax.all_to_all(many, axis, 0, 0, axis_index_groups=groups)


def body(gram_panel, left_factor, solved_prev, right_block):
    row_count = lax.axis_size("row")
    col_count = lax.axis_size("col")
    row_place = lax.axis_index("row")
    col_place = lax.axis_index("col")
    block_rows = right_block.shape[0]
    col_width = gram_panel.shape[1]
    panel = block_rows * row_count
    depth = left_factor.shape[1]
    wide = 4
    tall = row_count // wide
    chips = col_count // 2
    x_place = row_place % wide
    along_x = [[y * wide + x for x in range(wide)] for y in range(tall)]
    along_y = [[y * wide + x for y in range(tall)] for x in range(wide)]
    along_z = [[z * 2 + core for z in range(chips)] for core in range(2)]
    own = left_factor[:block_rows]
    per_col = row_count // col_count
    lane = lax.broadcasted_iota(jnp.int32, (1, panel), 1)

    prev_rows, vox = solved_prev.shape
    vox_part = vox // per_col
    packed = jnp.concatenate([solved_prev] + split_three(right_block), axis=0)
    pieces = []
    for turn in range(per_col):
        half = (row_place + turn) % per_col
        sent = lax.dynamic_slice_in_dim(packed, half * vox_part, vox_part, 1)
        pairs = []
        for r in range(row_count):
            for c in range(col_count):
                to_row = per_col * c + (r + turn) % per_col
                pairs.append((r * col_count + c, to_row * col_count + r // per_col))
        pieces.append(lax.ppermute(sent, ("row", "col"), pairs))
    flip = (row_place % per_col) == 1
    first = jnp.where(flip, pieces[1], pieces[0])
    second = jnp.where(flip, pieces[0], pieces[1])
    solved_here = jnp.concatenate([first[:prev_rows], second[:prev_rows]], axis=0)
    right_here = jnp.concatenate([first[prev_rows:], second[prev_rows:]], axis=0).astype(jnp.float32)
    right_here = right_here.reshape(per_col, 3, block_rows, vox_part)
    right_here = (right_here[:, 0] + right_here[:, 1] + right_here[:, 2]).reshape(col_width, vox_part)

    from_y = collect(own, "row", tall, along_y)
    packed = jnp.concatenate([own] + split_three(gram_panel[:block_rows]), axis=1)
    packed, from_y = lax.optimization_barrier((packed, from_y))
    from_x = collect(packed, "row", wide, along_x)
    rows_x = from_x[:, :, :depth].reshape(wide * block_rows, depth)
    rows_y = from_y.reshape(tall * block_rows, depth)
    gram_x = from_x[:, :, depth:].astype(jnp.float32).reshape(wide * block_rows, 3, per_col, block_rows)
    gram_x = gram_x[:, 0] + gram_x[:, 1] + gram_x[:, 2]
    per_x = wide // per_col
    gram_own = lax.dynamic_index_in_dim(gram_x, x_place % per_col, 1, keepdims=False)
    has_gram = (col_place % per_x) == (x_place // per_col)
    y_at = lax.broadcasted_iota(jnp.int32, (tall, 1, 1), 0)
    placed = jnp.where(has_gram & (y_at == col_place // per_x), gram_own.T[None], 0.0)
    partial = placed.reshape(tall * block_rows, wide * block_rows) - lax.dot_general(
        rows_y, rows_x, (((1,), (1,)), ((), ())), preferred_element_type=jnp.float32
    )
    kept = tall // 2 + 1
    turned = partial.reshape(tall, block_rows, wide * block_rows)[::-1]
    turned = lax.dynamic_slice_in_dim(jnp.concatenate([turned, turned], axis=0), tall - 1 - row_place // wide, tall, 0)
    thin = tall * block_rows // col_count
    partial = turned.reshape(col_count, thin, wide * block_rows)
    own_diag = jnp.sum(lax.all_to_all(partial, "col", 0, 0), axis=0)
    diag_z = collect(own_diag, "col", chips, along_z)

    chosen = lax.all_gather(rows_y, "row", axis=0, tiled=False, axis_index_groups=along_x)
    chosen = chosen.reshape(wide, tall, block_rows, depth).transpose(1, 0, 2, 3).reshape(panel, depth)
    at_col = lane // col_width == col_place
    gram_placed = jnp.where(at_col, jnp.tile(gram_panel, (1, col_count)), 0.0)
    update_part = gram_placed - lax.dot_general(
        left_factor, chosen, (((1,), (1,)), ((), ())), preferred_element_type=jnp.float32
    )
    right_placed = jnp.where(at_col, jnp.tile(right_here.T, (1, col_count)), 0.0)
    product = right_placed - lax.dot_general(
        solved_here, chosen, (((0,), (1,)), ((), ())), preferred_element_type=jnp.float32
    )

    diag_z, update_part, product = lax.optimization_barrier((diag_z[:kept], update_part, product))
    diag_row = collect(diag_z, "row", row_count)
    other = lax.ppermute(diag_row, "col", [(i, i ^ 1) for i in range(col_count)])
    update = lax.psum_scatter(update_part, "col", scatter_dimension=0, tiled=True)
    product = product.reshape(col_count, vox_part // col_count, panel)
    product, _ = lax.optimization_barrier((product, diag_row))
    spread_out = lax.all_to_all(product, "col", 0, 0)

    factored = factor((col_place % 2).reshape(1), diag_row, other, panel)
    factored, spread_out, update = lax.optimization_barrier((factored, spread_out, update))
    rows_out, vox_out = forward(factored, update, jnp.sum(spread_out, axis=0))

    pairs = []
    for r in range(row_count):
        for c in range(col_count):
            pairs.append((r * col_count + c, (per_col * c + r % per_col) * col_count + r // per_col))
    vox_out = lax.ppermute(vox_out, ("row", "col"), pairs)
    rows_out = rows_out.reshape(-1, col_count, col_width).transpose(1, 0, 2)
    panel_factor = lax.all_to_all(rows_out, "col", 0, 0).reshape(-1, col_width)
    vox_out, panel_factor = lax.optimization_barrier((vox_out, panel_factor))
    vox_out = vox_out.reshape(-1, row_count, block_rows).transpose(1, 0, 2)
    vox_out = lax.all_to_all(vox_out, "row", 0, 0).reshape(col_count, per_col, -1, block_rows)
    solved_panel = vox_out.transpose(1, 0, 2, 3).reshape(vox, block_rows).T
    return (panel_factor, solved_panel)


def solution(mesh):
    in_specs = (P("row", "col"), P("row", "col"), P("row", "col"), P("row", "col"))
    out_specs = (P("row", "col"), P("row", "col"))
    return jax.shard_map(body, mesh=mesh, in_specs=in_specs, out_specs=out_specs, check_vma=False)
```

```python
import jax
import jax.numpy as jnp
from jax import lax
from jax.experimental import pallas as pl
from jax.experimental.pallas import tpu as pltpu
from jax.sharding import PartitionSpec as P

HI = lax.Precision.HIGHEST


def factor_block(s_ref, c_ref):
    lane = lax.broadcasted_iota(jnp.int32, (8, 128), 1)
    sub = lax.broadcasted_iota(jnp.int32, (8, 128), 0)

    def wide(value, at):
        return jnp.broadcast_to(value[:, at:at + 1], (8, 128))

    def apply(v, base, q):
        rows = s_ref[8 * v:8 * v + 8, :]
        part = [wide(rows, base + j) * q[j] for j in range(8)]
        total = ((part[0] + part[1]) + (part[2] + part[3])) + ((part[4] + part[5]) + (part[6] + part[7]))
        rows = jnp.where((lane >= base) & (lane < base + 8), 0.0, rows) - total
        s_ref[8 * v:8 * v + 8, :] = rows
        return rows

    w = s_ref[0:8, :]
    follow = s_ref[8:16, :]
    waiting = []
    for g in range(16):
        base = 8 * g
        inside = (lane >= base) & (lane < base + 8)
        x = [[None] * 8 for _ in range(8)]
        for j in range(8):
            c = wide(w, base + j)
            at = 72 * (g % 2) + 8 * j
            c_ref[at:at + 8, :] = c
            for i in range(j, 8):
                x[i][j] = c_ref[pl.ds(at + i, 8, stride=0), :]
        start = jnp.where(lane == sub + base, 1.0, jnp.where(inside, 0.0, w))
        at = 72 * (g % 2) + 64
        c_ref[at:at + 8, :] = start
        r = [c_ref[pl.ds(at + j, 8, stride=0), :] for j in range(8)]
        if g < 15:
            if waiting:
                follow = waiting.pop(0)()
            b = [wide(follow, base + k) for k in range(8)]
            follow = jnp.where(inside, 0.0, follow)
        ahead = [[None] * 8 for _ in range(8)]
        top = None
        share = -(-len(waiting) // 8)
        for j in range(8):
            d = 1.0 / x[j][j]
            s = lax.rsqrt(x[j][j])
            t = r[j] * s
            top = t if top is None else jnp.where(sub == j, t, top)
            f = {i: x[i][j] * d for i in range(j + 1, 8)}
            for i in range(j + 1, 8):
                for k in range(j + 1, i + 1):
                    x[i][k] = x[i][k] - (x[i][j] * x[k][j]) * d if i == j + 1 else x[i][k] - f[i] * x[k][j]
            p = r[j] * d
            for i in range(j + 1, 8):
                r[i] = r[i] - x[i][j] * p
            if g < 15:
                follow = follow - b[j] * p
                for k in range(j + 1, 8):
                    b[k] = b[k] - b[j] * f[k]
            for i in range(j):
                r[i] = r[i] - ahead[i][j] * p
                for k in range(j + 1, 8):
                    ahead[i][k] = ahead[i][k] - ahead[i][j] * f[k]
            r[j] = p
            for k in range(j + 1, 8):
                ahead[j][k] = f[k]
            for _ in range(share):
                if waiting:
                    waiting.pop(0)()
        s_ref[base:base + 8, :] = top
        w = follow
        waiting = [lambda v=v, base=base, q=r: apply(v, base, q) for v in range(g + 2, 16)]
    rows = lax.broadcasted_iota(jnp.int32, (128, 128), 0)
    cols = lax.broadcasted_iota(jnp.int32, (128, 128), 1)
    s_ref[...] = jnp.where(cols <= rows, s_ref[...], 0.0)


def mm(a, b):
    return lax.dot_general(a, b, (((1,), (0,)), ((), ())), precision=HI, preferred_element_type=jnp.float32)


def mtm(a, b):
    return lax.dot_general(a, b, (((0,), (0,)), ((), ())), precision=HI, preferred_element_type=jnp.float32)


def mmt(a, b):
    return lax.dot_general(a, b, (((1,), (1,)), ((), ())), precision=HI, preferred_element_type=jnp.float32)


def factor_kernel(core_ref, mine_ref, other_ref, out_ref, w_ref, s_ref, m_ref, c_ref, sems):
    big, n, _ = w_ref.shape
    rows, kept, half, lanes = mine_ref.shape
    tall = n // lanes
    wide = rows // tall
    core = core_ref[0]
    for y in range(tall):
        for d in range(kept):
            z = y - d
            if z < 0 and d * 2 >= tall:
                continue
            for x in range(wide):
                at = (wide * max(z, 0) + x) * 2 * half
                first = pl.ds(pl.multiple_of(at + core * half, half), half)
                second = pl.ds(pl.multiple_of(at + (1 - core) * half, half), half)
                if z >= 0:
                    cols = slice((y % 2) * lanes, (y % 2) * lanes + lanes)
                    w_ref[y // 2, first, cols] = mine_ref[wide * y + x, d]
                    w_ref[y // 2, second, cols] = other_ref[wide * y + x, d]
                else:
                    s_ref[first, :] = mine_ref[wide * y + x, d]
                    s_ref[second, :] = other_ref[wide * y + x, d]
            if z < 0:
                z += tall
                cols = slice((z % 2) * lanes, (z % 2) * lanes + lanes)
                w_ref[z // 2, y * lanes:(y + 1) * lanes, cols] = s_ref[...].T

    def step(b, carry):
        top = pl.multiple_of(b * 256, 256)
        mid = pl.multiple_of(b * 256 + 128, 128)

        def half_step(h, carry):
            @pl.when(h == 0)
            def _():
                s_ref[...] = w_ref[b, pl.ds(top, 128), 0:128]

            @pl.when(h == 1)
            def _():
                m_ref[0:128, 0:128] = s_ref[...]
                upper = mm(s_ref[...], w_ref[b, pl.ds(top, 128), 128:256])
                m_ref[0:128, 128:256] = upper
                s_ref[...] = w_ref[b, pl.ds(mid, 128), 128:256] - mtm(upper, upper)

            factor_block(s_ref, c_ref)
            return carry

        lax.fori_loop(0, 2, half_step, 0)
        lower = mtm(m_ref[0:128, 128:256], m_ref[0:128, 0:128])
        m_ref[128:256, 0:128] = -mm(s_ref[...], lower)
        m_ref[0:128, 128:256] = jnp.zeros((128, 128), jnp.float32)
        m_ref[128:256, 128:256] = s_ref[...]
        w_ref[b, pl.ds(top, 256), :] = m_ref[...]

        for j in range(1, big):
            @pl.when(j > b)
            def _():
                w_ref[j, pl.ds(top, 256), :] = mm(m_ref[...], w_ref[j, pl.ds(top, 256), :])

        for j in range(big):
            @pl.when(j >= b)
            def _():
                pltpu.make_async_copy(
                    w_ref.at[j, pl.ds(top, 256), :], out_ref.at[j, pl.ds(top, 256), :], sems.at[b, j]
                ).start()

        def below(i, carry):
            at = pl.multiple_of(i * 256, 256)
            for j in range(1, big):
                @pl.when(j >= i)
                def _():
                    w_ref[j, pl.ds(at, 256), :] = w_ref[j, pl.ds(at, 256), :] - mtm(
                        w_ref[i, pl.ds(top, 256), :], w_ref[j, pl.ds(top, 256), :]
                    )
            return carry

        lax.fori_loop(b + 1, big, below, 0)
        return carry

    lax.fori_loop(0, big, step, 0)
    for b in range(big):
        span = pl.ds(256 * b, 256)
        for j in range(b, big):
            pltpu.make_async_copy(w_ref.at[j, span, :], out_ref.at[j, span, :], sems.at[b, j]).wait()


def solve_kernel(from_ref, u_ref, v_ref, out_u_ref, out_v_ref, w_ref, x_ref, sems):
    big = w_ref.shape[0]
    n = u_ref.shape[0]
    copies = {}
    for b in range(big):
        span = pl.ds(256 * b, 256)
        for j in range(b, big):
            copies[b, j] = pltpu.make_async_copy(from_ref.at[j, span, :], w_ref.at[j, span, :], sems.at[b, j])
            copies[b, j].start()
    x_ref[0:n, :] = u_ref[...]
    x_ref[n:, :] = v_ref[...]
    for b in range(big):
        span = slice(256 * b, 256 * b + 256)
        copies[b, b].wait()
        y = mmt(x_ref[:, span], w_ref[b, span, :])
        out_u_ref[:, span] = y[0:n, :]
        out_v_ref[:, span] = y[n:, :]
        for j in range(b + 1, big):
            right = slice(256 * j, 256 * j + 256)
            copies[b, j].wait()
            x_ref[:, right] = x_ref[:, right] - mm(y, w_ref[j, span, :])


def factor(core, mine, other, panel):
    vmem = pl.BlockSpec(memory_space=pltpu.VMEM)
    big = panel // 256
    return pl.pallas_call(
        factor_kernel,
        out_shape=pltpu.HBM((big, panel, 256), jnp.float32),
        in_specs=[pl.BlockSpec(memory_space=pltpu.SMEM), vmem, vmem],
        out_specs=pl.BlockSpec(memory_space=pltpu.HBM),
        scratch_shapes=[
            pltpu.VMEM((big, panel, 256), jnp.float32),
            pltpu.VMEM((128, 128), jnp.float32),
            pltpu.VMEM((256, 256), jnp.float32),
            pltpu.VMEM((144, 128), jnp.float32),
            pltpu.SemaphoreType.DMA((big, big)),
        ],
        compiler_params=pltpu.CompilerParams(vmem_limit_bytes=16 * 1024 * 1024),
        cost_estimate=pl.CostEstimate(flops=panel**3, transcendentals=0, bytes_accessed=8 * panel * panel),
    )(core, mine, other)


def forward(w, u, v):
    vmem = pl.BlockSpec(memory_space=pltpu.VMEM)
    return pl.pallas_call(
        solve_kernel,
        out_shape=[jax.ShapeDtypeStruct(u.shape, jnp.float32), jax.ShapeDtypeStruct(v.shape, jnp.float32)],
        in_specs=[pl.BlockSpec(memory_space=pltpu.HBM), vmem, vmem],
        out_specs=[vmem, vmem],
        scratch_shapes=[
            pltpu.VMEM(w.shape, jnp.float32),
            pltpu.VMEM((u.shape[0] + v.shape[0], u.shape[1]), jnp.float32),
            pltpu.SemaphoreType.DMA((w.shape[0], w.shape[0])),
        ],
        compiler_params=pltpu.CompilerParams(vmem_limit_bytes=12 * 1024 * 1024),
    )(pltpu.with_memory_space_constraint(w, pltpu.HBM), u, v)


def split_three(value):
    high = lax.reduce_precision(value, 8, 7)
    rest = value - high
    middle = lax.reduce_precision(rest, 8, 7)
    return [part.astype(jnp.bfloat16) for part in (high, middle, rest - middle)]


def collect(value, axis, count, groups=None):
    many = jnp.broadcast_to(value[None], (count,) + value.shape)
    return lax.all_to_all(many, axis, 0, 0, axis_index_groups=groups)


def body(gram_panel, left_factor, solved_prev, right_block):
    row_count = lax.axis_size("row")
    col_count = lax.axis_size("col")
    row_place = lax.axis_index("row")
    col_place = lax.axis_index("col")
    block_rows = right_block.shape[0]
    col_width = gram_panel.shape[1]
    panel = block_rows * row_count
    depth = left_factor.shape[1]
    wide = 4
    tall = row_count // wide
    chips = col_count // 2
    x_place = row_place % wide
    along_x = [[y * wide + x for x in range(wide)] for y in range(tall)]
    along_y = [[y * wide + x for y in range(tall)] for x in range(wide)]
    along_z = [[z * 2 + core for z in range(chips)] for core in range(2)]
    own = left_factor[:block_rows]
    per_col = row_count // col_count
    lane = lax.broadcasted_iota(jnp.int32, (1, panel), 1)

    prev_rows, vox = solved_prev.shape
    vox_part = vox // per_col
    packed = jnp.concatenate([solved_prev] + split_three(right_block), axis=0)
    spread = 2
    piece_vox = vox_part // spread
    sends = []
    routes = []
    for turn in range(per_col):
        half = (row_place + turn) % per_col
        for q in range(spread):
            sends.append(lax.dynamic_slice_in_dim(packed, half * vox_part + q * piece_vox, piece_vox, 1))
            pairs = []
            for r in range(row_count):
                for c in range(col_count):
                    to_row = per_col * c + (r + turn) % per_col + q * (row_count // spread)
                    pairs.append((r * col_count + c, to_row % row_count * col_count + r // per_col))
            routes.append(pairs)
    own, *sends = lax.optimization_barrier((own, *sends))
    parts = [lax.ppermute(sent, ("row", "col"), pairs) for sent, pairs in zip(sends, routes)]
    from_y, *parts = lax.optimization_barrier((collect(own, "row", tall, along_y), *parts))
    pieces = [jnp.concatenate(parts[turn * spread:(turn + 1) * spread], axis=1) for turn in range(per_col)]
    flip = (row_place % per_col) == 1
    first = jnp.where(flip, pieces[1], pieces[0])
    second = jnp.where(flip, pieces[0], pieces[1])
    solved_here = jnp.concatenate([first[:prev_rows], second[:prev_rows]], axis=0)
    right_here = jnp.concatenate([first[prev_rows:], second[prev_rows:]], axis=0).astype(jnp.float32)
    right_here = right_here.reshape(per_col, 3, block_rows, vox_part)
    right_here = (right_here[:, 0] + right_here[:, 1] + right_here[:, 2]).reshape(col_width, vox_part)

    packed = jnp.concatenate([own] + split_three(gram_panel[:block_rows]), axis=1)
    packed, from_y = lax.optimization_barrier((packed, from_y))
    from_x = collect(packed, "row", wide, along_x)
    rows_x = from_x[:, :, :depth].reshape(wide * block_rows, depth)
    rows_y = from_y.reshape(tall * block_rows, depth)
    gram_x = from_x[:, :, depth:].astype(jnp.float32).reshape(wide * block_rows, 3, per_col, block_rows)
    gram_x = gram_x[:, 0] + gram_x[:, 1] + gram_x[:, 2]
    per_x = wide // per_col
    gram_own = lax.dynamic_index_in_dim(gram_x, x_place % per_col, 1, keepdims=False)
    has_gram = (col_place % per_x) == (x_place // per_col)
    y_at = lax.broadcasted_iota(jnp.int32, (tall, 1, 1), 0)
    placed = jnp.where(has_gram & (y_at == col_place // per_x), gram_own.T[None], 0.0)
    partial = placed.reshape(tall * block_rows, wide * block_rows) - lax.dot_general(
        rows_y, rows_x, (((1,), (1,)), ((), ())), preferred_element_type=jnp.float32
    )
    kept = tall // 2 + 1
    turned = partial.reshape(tall, block_rows, wide * block_rows)[::-1]
    turned = lax.dynamic_slice_in_dim(jnp.concatenate([turned, turned], axis=0), tall - 1 - row_place // wide, tall, 0)
    thin = tall * block_rows // col_count
    partial = turned.reshape(col_count, thin, wide * block_rows)
    own_diag = jnp.sum(lax.all_to_all(partial, "col", 0, 0), axis=0)
    diag_z = collect(own_diag, "col", chips, along_z)

    chosen = lax.all_gather(rows_y, "row", axis=0, tiled=False, axis_index_groups=along_x)
    chosen = chosen.reshape(wide, tall, block_rows, depth).transpose(1, 0, 2, 3).reshape(panel, depth)
    at_col = lane // col_width == col_place
    gram_placed = jnp.where(at_col, jnp.tile(gram_panel, (1, col_count)), 0.0)
    update_part = gram_placed - lax.dot_general(
        left_factor, chosen, (((1,), (1,)), ((), ())), preferred_element_type=jnp.float32
    )
    right_placed = jnp.where(at_col, jnp.tile(right_here.T, (1, col_count)), 0.0)
    product = right_placed - lax.dot_general(
        solved_here, chosen, (((0,), (1,)), ((), ())), preferred_element_type=jnp.float32
    )

    diag_z, update_part, product = lax.optimization_barrier((diag_z[:kept], update_part, product))
    diag_row = collect(diag_z, "row", row_count)
    other = lax.ppermute(diag_row, "col", [(i, i ^ 1) for i in range(col_count)])
    update = lax.psum_scatter(update_part, "col", scatter_dimension=0, tiled=True)
    product = product.reshape(col_count, vox_part // col_count, panel)
    product, _ = lax.optimization_barrier((product, diag_row))
    spread_out = lax.all_to_all(product, "col", 0, 0)

    factored = factor((col_place % 2).reshape(1), diag_row, other, panel)
    factored, spread_out, update = lax.optimization_barrier((factored, spread_out, update))
    rows_out, vox_out = forward(factored, update, jnp.sum(spread_out, axis=0))

    pairs = []
    for r in range(row_count):
        for c in range(col_count):
            from_row = (r - c * spread // col_count * (row_count // spread)) % row_count
            pairs.append((r * col_count + c, (r % per_col * col_count + c) * col_count + from_row // per_col))
    vox_out = lax.ppermute(vox_out, ("row", "col"), pairs)
    rows_out = rows_out.reshape(-1, col_count, col_width).transpose(1, 0, 2)
    panel_factor = lax.all_to_all(rows_out, "col", 0, 0).reshape(-1, col_width)
    vox_out, panel_factor = lax.optimization_barrier((vox_out, panel_factor))
    vox_out = vox_out.reshape(-1, row_count, block_rows).transpose(1, 0, 2)
    solved_panel = lax.all_to_all(vox_out, "row", 0, 0).reshape(vox, block_rows).T
    return (panel_factor, solved_panel)


def solution(mesh):
    in_specs = (P("row", "col"), P("row", "col"), P("row", "col"), P("row", "col"))
    out_specs = (P("row", "col"), P("row", "col"))
    return jax.shard_map(body, mesh=mesh, in_specs=in_specs, out_specs=out_specs, check_vma=False)
```

```python
import jax
import jax.numpy as jnp
from jax import lax
from jax.experimental import pallas as pl
from jax.experimental.pallas import tpu as pltpu
from jax.sharding import PartitionSpec as P

HI = lax.Precision.HIGHEST


def factor_block(s_ref, c_ref):
    lane = lax.broadcasted_iota(jnp.int32, (8, 128), 1)
    sub = lax.broadcasted_iota(jnp.int32, (8, 128), 0)

    def wide(value, at):
        return jnp.broadcast_to(value[:, at:at + 1], (8, 128))

    def apply(v, base, q):
        rows = s_ref[8 * v:8 * v + 8, :]
        part = [wide(rows, base + j) * q[j] for j in range(8)]
        total = ((part[0] + part[1]) + (part[2] + part[3])) + ((part[4] + part[5]) + (part[6] + part[7]))
        rows = jnp.where((lane >= base) & (lane < base + 8), 0.0, rows) - total
        s_ref[8 * v:8 * v + 8, :] = rows
        return rows

    w = s_ref[0:8, :]
    follow = s_ref[8:16, :]
    waiting = []
    for g in range(16):
        base = 8 * g
        inside = (lane >= base) & (lane < base + 8)
        x = [[None] * 8 for _ in range(8)]
        for j in range(8):
            c = wide(w, base + j)
            at = 72 * (g % 2) + 8 * j
            c_ref[at:at + 8, :] = c
            for i in range(j, 8):
                x[i][j] = c_ref[pl.ds(at + i, 8, stride=0), :]
        start = jnp.where(lane == sub + base, 1.0, jnp.where(inside, 0.0, w))
        at = 72 * (g % 2) + 64
        c_ref[at:at + 8, :] = start
        r = [c_ref[pl.ds(at + j, 8, stride=0), :] for j in range(8)]
        if g < 15:
            if waiting:
                follow = waiting.pop(0)()
            b = [wide(follow, base + k) for k in range(8)]
            follow = jnp.where(inside, 0.0, follow)
        ahead = [[None] * 8 for _ in range(8)]
        top = None
        share = -(-len(waiting) // 8)
        for j in range(8):
            d = 1.0 / x[j][j]
            s = lax.rsqrt(x[j][j])
            t = r[j] * s
            top = t if top is None else jnp.where(sub == j, t, top)
            f = {i: x[i][j] * d for i in range(j + 1, 8)}
            for i in range(j + 1, 8):
                for k in range(j + 1, i + 1):
                    x[i][k] = x[i][k] - (x[i][j] * x[k][j]) * d if i == j + 1 else x[i][k] - f[i] * x[k][j]
            p = r[j] * d
            for i in range(j + 1, 8):
                r[i] = r[i] - x[i][j] * p
            if g < 15:
                follow = follow - b[j] * p
                for k in range(j + 1, 8):
                    b[k] = b[k] - b[j] * f[k]
            for i in range(j):
                r[i] = r[i] - ahead[i][j] * p
                for k in range(j + 1, 8):
                    ahead[i][k] = ahead[i][k] - ahead[i][j] * f[k]
            r[j] = p
            for k in range(j + 1, 8):
                ahead[j][k] = f[k]
            for _ in range(share):
                if waiting:
                    waiting.pop(0)()
        s_ref[base:base + 8, :] = top
        w = follow
        waiting = [lambda v=v, base=base, q=r: apply(v, base, q) for v in range(g + 2, 16)]
    rows = lax.broadcasted_iota(jnp.int32, (128, 128), 0)
    cols = lax.broadcasted_iota(jnp.int32, (128, 128), 1)
    s_ref[...] = jnp.where(cols <= rows, s_ref[...], 0.0)


def mm(a, b):
    return lax.dot_general(a, b, (((1,), (0,)), ((), ())), precision=HI, preferred_element_type=jnp.float32)


def mtm(a, b):
    return lax.dot_general(a, b, (((0,), (0,)), ((), ())), precision=HI, preferred_element_type=jnp.float32)


def mmt(a, b):
    return lax.dot_general(a, b, (((1,), (1,)), ((), ())), precision=HI, preferred_element_type=jnp.float32)


def factor_kernel(core_ref, mine_ref, other_ref, out_ref, w_ref, s_ref, m_ref, c_ref, sems):
    big, n, _ = w_ref.shape
    rows, kept, half, lanes = mine_ref.shape
    tall = n // lanes
    wide = rows // tall
    core = core_ref[0]
    for y in range(tall):
        for d in range(kept):
            z = y - d
            if z < 0 and d * 2 >= tall:
                continue
            for x in range(wide):
                at = (wide * max(z, 0) + x) * 2 * half
                first = pl.ds(pl.multiple_of(at + core * half, half), half)
                second = pl.ds(pl.multiple_of(at + (1 - core) * half, half), half)
                if z >= 0:
                    cols = slice((y % 2) * lanes, (y % 2) * lanes + lanes)
                    w_ref[y // 2, first, cols] = mine_ref[wide * y + x, d]
                    w_ref[y // 2, second, cols] = other_ref[wide * y + x, d]
                else:
                    s_ref[first, :] = mine_ref[wide * y + x, d]
                    s_ref[second, :] = other_ref[wide * y + x, d]
            if z < 0:
                z += tall
                cols = slice((z % 2) * lanes, (z % 2) * lanes + lanes)
                w_ref[z // 2, y * lanes:(y + 1) * lanes, cols] = s_ref[...].T

    def step(b, carry):
        top = pl.multiple_of(b * 256, 256)
        mid = pl.multiple_of(b * 256 + 128, 128)

        def half_step(h, carry):
            @pl.when(h == 0)
            def _():
                s_ref[...] = w_ref[b, pl.ds(top, 128), 0:128]

            @pl.when(h == 1)
            def _():
                m_ref[0:128, 0:128] = s_ref[...]
                upper = mm(s_ref[...], w_ref[b, pl.ds(top, 128), 128:256])
                m_ref[0:128, 128:256] = upper
                s_ref[...] = w_ref[b, pl.ds(mid, 128), 128:256] - mtm(upper, upper)

            factor_block(s_ref, c_ref)
            return carry

        lax.fori_loop(0, 2, half_step, 0)
        lower = mtm(m_ref[0:128, 128:256], m_ref[0:128, 0:128])
        m_ref[128:256, 0:128] = -mm(s_ref[...], lower)
        m_ref[0:128, 128:256] = jnp.zeros((128, 128), jnp.float32)
        m_ref[128:256, 128:256] = s_ref[...]
        w_ref[b, pl.ds(top, 256), :] = m_ref[...]

        for j in range(1, big):
            @pl.when(j > b)
            def _():
                w_ref[j, pl.ds(top, 256), :] = mm(m_ref[...], w_ref[j, pl.ds(top, 256), :])

        for j in range(big):
            @pl.when(j >= b)
            def _():
                pltpu.make_async_copy(
                    w_ref.at[j, pl.ds(top, 256), :], out_ref.at[j, pl.ds(top, 256), :], sems.at[b, j]
                ).start()

        def below(i, carry):
            at = pl.multiple_of(i * 256, 256)
            for j in range(1, big):
                @pl.when(j >= i)
                def _():
                    w_ref[j, pl.ds(at, 256), :] = w_ref[j, pl.ds(at, 256), :] - mtm(
                        w_ref[i, pl.ds(top, 256), :], w_ref[j, pl.ds(top, 256), :]
                    )
            return carry

        lax.fori_loop(b + 1, big, below, 0)
        return carry

    lax.fori_loop(0, big, step, 0)
    for b in range(big):
        span = pl.ds(256 * b, 256)
        for j in range(b, big):
            pltpu.make_async_copy(w_ref.at[j, span, :], out_ref.at[j, span, :], sems.at[b, j]).wait()


def solve_kernel(from_ref, u_ref, v_ref, out_u_ref, out_v_ref, w_ref, x_ref, sems):
    big = w_ref.shape[0]
    n = u_ref.shape[0]
    copies = {}
    for b in range(big):
        span = pl.ds(256 * b, 256)
        for j in range(b, big):
            copies[b, j] = pltpu.make_async_copy(from_ref.at[j, span, :], w_ref.at[j, span, :], sems.at[b, j])
            copies[b, j].start()
    x_ref[0:n, :] = u_ref[...]
    x_ref[n:, :] = v_ref[...]
    for b in range(big):
        span = slice(256 * b, 256 * b + 256)
        copies[b, b].wait()
        y = mmt(x_ref[:, span], w_ref[b, span, :])
        out_u_ref[:, span] = y[0:n, :]
        out_v_ref[:, span] = y[n:, :]
        for j in range(b + 1, big):
            right = slice(256 * j, 256 * j + 256)
            copies[b, j].wait()
            x_ref[:, right] = x_ref[:, right] - mm(y, w_ref[j, span, :])


def factor(core, mine, other, panel):
    vmem = pl.BlockSpec(memory_space=pltpu.VMEM)
    big = panel // 256
    return pl.pallas_call(
        factor_kernel,
        out_shape=pltpu.HBM((big, panel, 256), jnp.float32),
        in_specs=[pl.BlockSpec(memory_space=pltpu.SMEM), vmem, vmem],
        out_specs=pl.BlockSpec(memory_space=pltpu.HBM),
        scratch_shapes=[
            pltpu.VMEM((big, panel, 256), jnp.float32),
            pltpu.VMEM((128, 128), jnp.float32),
            pltpu.VMEM((256, 256), jnp.float32),
            pltpu.VMEM((144, 128), jnp.float32),
            pltpu.SemaphoreType.DMA((big, big)),
        ],
        compiler_params=pltpu.CompilerParams(vmem_limit_bytes=16 * 1024 * 1024),
        cost_estimate=pl.CostEstimate(flops=panel**3, transcendentals=0, bytes_accessed=8 * panel * panel),
    )(core, mine, other)


def forward(w, u, v):
    vmem = pl.BlockSpec(memory_space=pltpu.VMEM)
    return pl.pallas_call(
        solve_kernel,
        out_shape=[jax.ShapeDtypeStruct(u.shape, jnp.float32), jax.ShapeDtypeStruct(v.shape, jnp.float32)],
        in_specs=[pl.BlockSpec(memory_space=pltpu.HBM), vmem, vmem],
        out_specs=[vmem, vmem],
        scratch_shapes=[
            pltpu.VMEM(w.shape, jnp.float32),
            pltpu.VMEM((u.shape[0] + v.shape[0], u.shape[1]), jnp.float32),
            pltpu.SemaphoreType.DMA((w.shape[0], w.shape[0])),
        ],
        compiler_params=pltpu.CompilerParams(vmem_limit_bytes=12 * 1024 * 1024),
    )(pltpu.with_memory_space_constraint(w, pltpu.HBM), u, v)


def split_three(value):
    high = lax.reduce_precision(value, 8, 7)
    rest = value - high
    middle = lax.reduce_precision(rest, 8, 7)
    return [part.astype(jnp.bfloat16) for part in (high, middle, rest - middle)]


def collect(value, axis, count, groups=None):
    many = jnp.broadcast_to(value[None], (count,) + value.shape)
    return lax.all_to_all(many, axis, 0, 0, axis_index_groups=groups)


def body(gram_panel, left_factor, solved_prev, right_block):
    row_count = lax.axis_size("row")
    col_count = lax.axis_size("col")
    row_place = lax.axis_index("row")
    col_place = lax.axis_index("col")
    block_rows = right_block.shape[0]
    col_width = gram_panel.shape[1]
    panel = block_rows * row_count
    depth = left_factor.shape[1]
    wide = 4
    tall = row_count // wide
    chips = col_count // 2
    x_place = row_place % wide
    along_x = [[y * wide + x for x in range(wide)] for y in range(tall)]
    along_y = [[y * wide + x for y in range(tall)] for x in range(wide)]
    along_z = [[z * 2 + core for z in range(chips)] for core in range(2)]
    own = left_factor[:block_rows]
    per_col = row_count // col_count
    lane = lax.broadcasted_iota(jnp.int32, (1, panel), 1)

    prev_rows, vox = solved_prev.shape
    vox_part = vox // per_col
    packed = jnp.concatenate([solved_prev] + split_three(right_block), axis=0)
    spread = 2
    piece_vox = vox_part // spread
    sends = []
    routes = []
    for turn in range(per_col):
        half = (row_place + turn) % per_col
        for q in range(spread):
            sends.append(lax.dynamic_slice_in_dim(packed, half * vox_part + q * piece_vox, piece_vox, 1))
            pairs = []
            for r in range(row_count):
                for c in range(col_count):
                    to_row = per_col * c + (r + turn) % per_col + q * (row_count // spread)
                    pairs.append((r * col_count + c, to_row % row_count * col_count + r // per_col))
            routes.append(pairs)
    parts = []

    def beside(stage, value):
        start, *sends[:] = lax.optimization_barrier((value, *sends))
        part = lax.ppermute(sends.pop(0), ("row", "col"), routes.pop(0))
        out, part, *sends[:] = lax.optimization_barrier((stage(start), part, *sends))
        parts.append(part)
        return out

    from_y = beside(lambda value: collect(value, "row", tall, along_y), own)
    packed = jnp.concatenate([own] + split_three(gram_panel[:block_rows]), axis=1)
    packed, from_y = lax.optimization_barrier((packed, from_y))
    from_x = beside(lambda value: collect(value, "row", wide, along_x), packed)
    rows_x = from_x[:, :, :depth].reshape(wide * block_rows, depth)
    rows_y = from_y.reshape(tall * block_rows, depth)
    gram_x = from_x[:, :, depth:].astype(jnp.float32).reshape(wide * block_rows, 3, per_col, block_rows)
    gram_x = gram_x[:, 0] + gram_x[:, 1] + gram_x[:, 2]
    per_x = wide // per_col
    gram_own = lax.dynamic_index_in_dim(gram_x, x_place % per_col, 1, keepdims=False)
    has_gram = (col_place % per_x) == (x_place // per_col)
    y_at = lax.broadcasted_iota(jnp.int32, (tall, 1, 1), 0)
    placed = jnp.where(has_gram & (y_at == col_place // per_x), gram_own.T[None], 0.0)
    partial = placed.reshape(tall * block_rows, wide * block_rows) - lax.dot_general(
        rows_y, rows_x, (((1,), (1,)), ((), ())), preferred_element_type=jnp.float32
    )
    kept = tall // 2 + 1
    turned = partial.reshape(tall, block_rows, wide * block_rows)[::-1]
    turned = lax.dynamic_slice_in_dim(jnp.concatenate([turned, turned], axis=0), tall - 1 - row_place // wide, tall, 0)
    thin = tall * block_rows // col_count
    partial = turned.reshape(col_count, thin, wide * block_rows)
    own_diag = jnp.sum(beside(lambda value: lax.all_to_all(value, "col", 0, 0), partial), axis=0)
    diag_z = beside(lambda value: collect(value, "col", chips, along_z), own_diag)
    pieces = [jnp.concatenate(parts[turn * spread:(turn + 1) * spread], axis=1) for turn in range(per_col)]
    flip = (row_place % per_col) == 1
    first = jnp.where(flip, pieces[1], pieces[0])
    second = jnp.where(flip, pieces[0], pieces[1])
    solved_here = jnp.concatenate([first[:prev_rows], second[:prev_rows]], axis=0)
    right_here = jnp.concatenate([first[prev_rows:], second[prev_rows:]], axis=0).astype(jnp.float32)
    right_here = right_here.reshape(per_col, 3, block_rows, vox_part)
    right_here = (right_here[:, 0] + right_here[:, 1] + right_here[:, 2]).reshape(col_width, vox_part)

    chosen = lax.all_gather(rows_y, "row", axis=0, tiled=False, axis_index_groups=along_x)
    chosen = chosen.reshape(wide, tall, block_rows, depth).transpose(1, 0, 2, 3).reshape(panel, depth)
    at_col = lane // col_width == col_place
    gram_placed = jnp.where(at_col, jnp.tile(gram_panel, (1, col_count)), 0.0)
    update_part = gram_placed - lax.dot_general(
        left_factor, chosen, (((1,), (1,)), ((), ())), preferred_element_type=jnp.float32
    )
    right_placed = jnp.where(at_col, jnp.tile(right_here.T, (1, col_count)), 0.0)
    product = right_placed - lax.dot_general(
        solved_here, chosen, (((0,), (1,)), ((), ())), preferred_element_type=jnp.float32
    )

    diag_row = collect(diag_z[:kept], "row", row_count)
    other = lax.ppermute(diag_row, "col", [(i, i ^ 1) for i in range(col_count)])
    update = lax.psum_scatter(update_part, "col", scatter_dimension=0, tiled=True)
    product = product.reshape(col_count, vox_part // col_count, panel)
    product, _ = lax.optimization_barrier((product, diag_row))
    spread_out = lax.all_to_all(product, "col", 0, 0)

    factored = factor((col_place % 2).reshape(1), diag_row, other, panel)
    factored, spread_out, update = lax.optimization_barrier((factored, spread_out, update))
    rows_out, vox_out = forward(factored, update, jnp.sum(spread_out, axis=0))

    vox_out = vox_out.reshape(-1, row_count, block_rows).transpose(1, 0, 2)
    vox_out = lax.all_to_all(vox_out, "row", 0, 0)
    start = col_place * spread // col_count * (row_count // spread)
    vox_out = lax.dynamic_slice_in_dim(jnp.concatenate([vox_out, vox_out], axis=0), start, row_count, 0)
    rows_out = rows_out.reshape(-1, col_count, col_width).transpose(1, 0, 2)
    count = rows_out.shape[1] * col_width
    both = jnp.concatenate([rows_out.reshape(col_count, count), vox_out.reshape(col_count, -1)], axis=1)
    both = lax.all_to_all(both.reshape(col_count, -1, 128), "col", 0, 0).reshape(col_count, -1)
    panel_factor = both[:, :count].reshape(-1, col_width)
    vox_out = both[:, count:].reshape(col_count, per_col, -1, block_rows).transpose(1, 0, 2, 3)
    solved_panel = vox_out.reshape(vox, block_rows).T
    return (panel_factor, solved_panel)


def solution(mesh):
    in_specs = (P("row", "col"), P("row", "col"), P("row", "col"), P("row", "col"))
    out_specs = (P("row", "col"), P("row", "col"))
    return jax.shard_map(body, mesh=mesh, in_specs=in_specs, out_specs=out_specs, check_vma=False)
```

```python
import jax
import jax.numpy as jnp
from jax import lax
from jax.experimental import pallas as pl
from jax.experimental.pallas import tpu as pltpu
from jax.sharding import PartitionSpec as P

HI = lax.Precision.HIGHEST


def factor_block(s_ref, c_ref):
    lane = lax.broadcasted_iota(jnp.int32, (8, 128), 1)
    sub = lax.broadcasted_iota(jnp.int32, (8, 128), 0)

    def wide(value, at):
        return jnp.broadcast_to(value[:, at:at + 1], (8, 128))

    def apply(v, base, q):
        rows = s_ref[8 * v:8 * v + 8, :]
        part = [wide(rows, base + j) * q[j] for j in range(8)]
        total = ((part[0] + part[1]) + (part[2] + part[3])) + ((part[4] + part[5]) + (part[6] + part[7]))
        rows = jnp.where((lane >= base) & (lane < base + 8), 0.0, rows) - total
        s_ref[8 * v:8 * v + 8, :] = rows
        return rows

    w = s_ref[0:8, :]
    follow = s_ref[8:16, :]
    waiting = []
    for g in range(16):
        base = 8 * g
        inside = (lane >= base) & (lane < base + 8)
        x = [[None] * 8 for _ in range(8)]
        for j in range(8):
            c = wide(w, base + j)
            at = 72 * (g % 2) + 8 * j
            c_ref[at:at + 8, :] = c
            for i in range(j, 8):
                x[i][j] = c_ref[pl.ds(at + i, 8, stride=0), :]
        start = jnp.where(lane == sub + base, 1.0, jnp.where(inside, 0.0, w))
        at = 72 * (g % 2) + 64
        c_ref[at:at + 8, :] = start
        r = [c_ref[pl.ds(at + j, 8, stride=0), :] for j in range(8)]
        if g < 15:
            if waiting:
                follow = waiting.pop(0)()
            b = [wide(follow, base + k) for k in range(8)]
            follow = jnp.where(inside, 0.0, follow)
        ahead = [[None] * 8 for _ in range(8)]
        top = None
        share = -(-len(waiting) // 8)
        for j in range(8):
            d = 1.0 / x[j][j]
            s = lax.rsqrt(x[j][j])
            t = r[j] * s
            top = t if top is None else jnp.where(sub == j, t, top)
            f = {i: x[i][j] * d for i in range(j + 1, 8)}
            for i in range(j + 1, 8):
                for k in range(j + 1, i + 1):
                    x[i][k] = x[i][k] - (x[i][j] * x[k][j]) * d if i == j + 1 else x[i][k] - f[i] * x[k][j]
            p = r[j] * d
            for i in range(j + 1, 8):
                r[i] = r[i] - x[i][j] * p
            if g < 15:
                follow = follow - b[j] * p
                for k in range(j + 1, 8):
                    b[k] = b[k] - b[j] * f[k]
            for i in range(j):
                r[i] = r[i] - ahead[i][j] * p
                for k in range(j + 1, 8):
                    ahead[i][k] = ahead[i][k] - ahead[i][j] * f[k]
            r[j] = p
            for k in range(j + 1, 8):
                ahead[j][k] = f[k]
            for _ in range(share):
                if waiting:
                    waiting.pop(0)()
        s_ref[base:base + 8, :] = top
        w = follow
        waiting = [lambda v=v, base=base, q=r: apply(v, base, q) for v in range(g + 2, 16)]
    rows = lax.broadcasted_iota(jnp.int32, (128, 128), 0)
    cols = lax.broadcasted_iota(jnp.int32, (128, 128), 1)
    s_ref[...] = jnp.where(cols <= rows, s_ref[...], 0.0)


def mm(a, b):
    return lax.dot_general(a, b, (((1,), (0,)), ((), ())), precision=HI, preferred_element_type=jnp.float32)


def mtm(a, b):
    return lax.dot_general(a, b, (((0,), (0,)), ((), ())), precision=HI, preferred_element_type=jnp.float32)


def mmt(a, b):
    return lax.dot_general(a, b, (((1,), (1,)), ((), ())), precision=HI, preferred_element_type=jnp.float32)


def factor_kernel(core_ref, mine_ref, other_ref, out_ref, w_ref, s_ref, m_ref, c_ref, sems):
    big, n, _ = w_ref.shape
    rows, kept, half, lanes = mine_ref.shape
    tall = n // lanes
    wide = rows // tall
    core = core_ref[0]
    for y in range(tall):
        for d in range(kept):
            z = y - d
            if z < 0 and d * 2 >= tall:
                continue
            for x in range(wide):
                at = (wide * max(z, 0) + x) * 2 * half
                first = pl.ds(pl.multiple_of(at + core * half, half), half)
                second = pl.ds(pl.multiple_of(at + (1 - core) * half, half), half)
                if z >= 0:
                    cols = slice((y % 2) * lanes, (y % 2) * lanes + lanes)
                    w_ref[y // 2, first, cols] = mine_ref[wide * y + x, d]
                    w_ref[y // 2, second, cols] = other_ref[wide * y + x, d]
                else:
                    s_ref[first, :] = mine_ref[wide * y + x, d]
                    s_ref[second, :] = other_ref[wide * y + x, d]
            if z < 0:
                z += tall
                cols = slice((z % 2) * lanes, (z % 2) * lanes + lanes)
                w_ref[z // 2, y * lanes:(y + 1) * lanes, cols] = s_ref[...].T

    def step(b, carry):
        top = pl.multiple_of(b * 256, 256)
        mid = pl.multiple_of(b * 256 + 128, 128)

        def half_step(h, carry):
            @pl.when(h == 0)
            def _():
                s_ref[...] = w_ref[b, pl.ds(top, 128), 0:128]

            @pl.when(h == 1)
            def _():
                m_ref[0:128, 0:128] = s_ref[...]
                upper = mm(s_ref[...], w_ref[b, pl.ds(top, 128), 128:256])
                m_ref[0:128, 128:256] = upper
                s_ref[...] = w_ref[b, pl.ds(mid, 128), 128:256] - mtm(upper, upper)

            factor_block(s_ref, c_ref)
            return carry

        lax.fori_loop(0, 2, half_step, 0)
        lower = mtm(m_ref[0:128, 128:256], m_ref[0:128, 0:128])
        m_ref[128:256, 0:128] = -mm(s_ref[...], lower)
        m_ref[0:128, 128:256] = jnp.zeros((128, 128), jnp.float32)
        m_ref[128:256, 128:256] = s_ref[...]
        w_ref[b, pl.ds(top, 256), :] = m_ref[...]

        for j in range(1, big):
            @pl.when(j > b)
            def _():
                w_ref[j, pl.ds(top, 256), :] = mm(m_ref[...], w_ref[j, pl.ds(top, 256), :])

        for j in range(big):
            @pl.when(j >= b)
            def _():
                pltpu.make_async_copy(
                    w_ref.at[j, pl.ds(top, 256), :], out_ref.at[j, pl.ds(top, 256), :], sems.at[b, j]
                ).start()

        def below(i, carry):
            at = pl.multiple_of(i * 256, 256)
            for j in range(1, big):
                @pl.when(j >= i)
                def _():
                    w_ref[j, pl.ds(at, 256), :] = w_ref[j, pl.ds(at, 256), :] - mtm(
                        w_ref[i, pl.ds(top, 256), :], w_ref[j, pl.ds(top, 256), :]
                    )
            return carry

        lax.fori_loop(b + 1, big, below, 0)
        return carry

    lax.fori_loop(0, big, step, 0)
    for b in range(big):
        span = pl.ds(256 * b, 256)
        for j in range(b, big):
            pltpu.make_async_copy(w_ref.at[j, span, :], out_ref.at[j, span, :], sems.at[b, j]).wait()


def solve_kernel(from_ref, u_ref, v_ref, out_u_ref, out_v_ref, w_ref, x_ref, sems):
    big = w_ref.shape[0]
    n = u_ref.shape[0]
    copies = {}
    for b in range(big):
        span = pl.ds(256 * b, 256)
        for j in range(b, big):
            copies[b, j] = pltpu.make_async_copy(from_ref.at[j, span, :], w_ref.at[j, span, :], sems.at[b, j])
            copies[b, j].start()
    x_ref[0:n, :] = u_ref[...]
    x_ref[n:, :] = v_ref[...]
    for b in range(big):
        span = slice(256 * b, 256 * b + 256)
        copies[b, b].wait()
        y = mmt(x_ref[:, span], w_ref[b, span, :])
        out_u_ref[:, span] = y[0:n, :]
        out_v_ref[:, span] = y[n:, :]
        for j in range(b + 1, big):
            right = slice(256 * j, 256 * j + 256)
            copies[b, j].wait()
            x_ref[:, right] = x_ref[:, right] - mm(y, w_ref[j, span, :])


def factor(core, mine, other, panel):
    vmem = pl.BlockSpec(memory_space=pltpu.VMEM)
    big = panel // 256
    return pl.pallas_call(
        factor_kernel,
        out_shape=pltpu.HBM((big, panel, 256), jnp.float32),
        in_specs=[pl.BlockSpec(memory_space=pltpu.SMEM), vmem, vmem],
        out_specs=pl.BlockSpec(memory_space=pltpu.HBM),
        scratch_shapes=[
            pltpu.VMEM((big, panel, 256), jnp.float32),
            pltpu.VMEM((128, 128), jnp.float32),
            pltpu.VMEM((256, 256), jnp.float32),
            pltpu.VMEM((144, 128), jnp.float32),
            pltpu.SemaphoreType.DMA((big, big)),
        ],
        compiler_params=pltpu.CompilerParams(vmem_limit_bytes=16 * 1024 * 1024),
        cost_estimate=pl.CostEstimate(flops=panel**3, transcendentals=0, bytes_accessed=8 * panel * panel),
    )(core, mine, other)


def forward(w, u, v):
    vmem = pl.BlockSpec(memory_space=pltpu.VMEM)
    return pl.pallas_call(
        solve_kernel,
        out_shape=[jax.ShapeDtypeStruct(u.shape, jnp.float32), jax.ShapeDtypeStruct(v.shape, jnp.float32)],
        in_specs=[pl.BlockSpec(memory_space=pltpu.HBM), vmem, vmem],
        out_specs=[vmem, vmem],
        scratch_shapes=[
            pltpu.VMEM(w.shape, jnp.float32),
            pltpu.VMEM((u.shape[0] + v.shape[0], u.shape[1]), jnp.float32),
            pltpu.SemaphoreType.DMA((w.shape[0], w.shape[0])),
        ],
        compiler_params=pltpu.CompilerParams(vmem_limit_bytes=12 * 1024 * 1024),
    )(pltpu.with_memory_space_constraint(w, pltpu.HBM), u, v)


def split_three(value):
    high = lax.reduce_precision(value, 8, 7)
    rest = value - high
    middle = lax.reduce_precision(rest, 8, 7)
    return [part.astype(jnp.bfloat16) for part in (high, middle, rest - middle)]


def collect(value, axis, count, groups=None):
    many = jnp.broadcast_to(value[None], (count,) + value.shape)
    return lax.all_to_all(many, axis, 0, 0, axis_index_groups=groups)


def body(gram_panel, left_factor, solved_prev, right_block):
    row_count = lax.axis_size("row")
    col_count = lax.axis_size("col")
    row_place = lax.axis_index("row")
    col_place = lax.axis_index("col")
    block_rows = right_block.shape[0]
    col_width = gram_panel.shape[1]
    panel = block_rows * row_count
    depth = left_factor.shape[1]
    wide = 4
    tall = row_count // wide
    chips = col_count // 2
    x_place = row_place % wide
    along_x = [[y * wide + x for x in range(wide)] for y in range(tall)]
    along_y = [[y * wide + x for y in range(tall)] for x in range(wide)]
    along_z = [[z * 2 + core for z in range(chips)] for core in range(2)]
    own = left_factor[:block_rows]
    per_col = row_count // col_count
    lane = lax.broadcasted_iota(jnp.int32, (1, panel), 1)

    prev_rows, vox = solved_prev.shape
    vox_part = vox // per_col
    packed = jnp.concatenate([solved_prev] + split_three(right_block), axis=0)
    spread = 2
    piece_vox = vox_part // spread
    sends = []
    routes = []
    for turn in range(per_col):
        half = (row_place + turn) % per_col
        for q in range(spread):
            sends.append(lax.dynamic_slice_in_dim(packed, half * vox_part + q * piece_vox, piece_vox, 1))
            pairs = []
            for r in range(row_count):
                for c in range(col_count):
                    to_row = per_col * c + (r + turn) % per_col + q * (row_count // spread)
                    pairs.append((r * col_count + c, to_row % row_count * col_count + r // per_col))
            routes.append(pairs)
    own, *sends = lax.optimization_barrier((own, *sends))
    parts = [lax.ppermute(sent, ("row", "col"), pairs) for sent, pairs in zip(sends, routes)]
    from_y, *parts = lax.optimization_barrier((collect(own, "row", tall, along_y), *parts))
    packed = jnp.concatenate([own] + split_three(gram_panel[:block_rows]), axis=1)
    packed, from_y = lax.optimization_barrier((packed, from_y))
    from_x = collect(packed, "row", wide, along_x)
    pieces = [jnp.concatenate(parts[turn * spread:(turn + 1) * spread], axis=1) for turn in range(per_col)]
    flip = (row_place % per_col) == 1
    first = jnp.where(flip, pieces[1], pieces[0])
    second = jnp.where(flip, pieces[0], pieces[1])
    solved_here = jnp.concatenate([first[:prev_rows], second[:prev_rows]], axis=0)
    right_here = jnp.concatenate([first[prev_rows:], second[prev_rows:]], axis=0).astype(jnp.float32)
    right_here = right_here.reshape(per_col, 3, block_rows, vox_part)
    right_here = (right_here[:, 0] + right_here[:, 1] + right_here[:, 2]).reshape(col_width, vox_part)
    rows_x = from_x[:, :, :depth].reshape(wide * block_rows, depth)
    rows_y = from_y.reshape(tall * block_rows, depth)
    gram_x = from_x[:, :, depth:].astype(jnp.float32).reshape(wide * block_rows, 3, per_col, block_rows)
    gram_x = gram_x[:, 0] + gram_x[:, 1] + gram_x[:, 2]
    per_x = wide // per_col
    gram_own = lax.dynamic_index_in_dim(gram_x, x_place % per_col, 1, keepdims=False)
    has_gram = (col_place % per_x) == (x_place // per_col)
    y_at = lax.broadcasted_iota(jnp.int32, (tall, 1, 1), 0)
    placed = jnp.where(has_gram & (y_at == col_place // per_x), gram_own.T[None], 0.0)
    partial = placed.reshape(tall * block_rows, wide * block_rows) - lax.dot_general(
        rows_y, rows_x, (((1,), (1,)), ((), ())), preferred_element_type=jnp.float32
    )
    kept = tall // 2 + 1
    turned = partial.reshape(tall, block_rows, wide * block_rows)[::-1]
    turned = lax.dynamic_slice_in_dim(jnp.concatenate([turned, turned], axis=0), tall - 1 - row_place // wide, tall, 0)
    thin = tall * block_rows // col_count
    partial = turned.reshape(col_count, thin, wide * block_rows)
    own_diag = jnp.sum(lax.all_to_all(partial, "col", 0, 0), axis=0)
    diag_z = collect(own_diag, "col", chips, along_z)

    chosen = lax.all_gather(rows_y, "row", axis=0, tiled=False, axis_index_groups=along_x)
    chosen = chosen.reshape(wide, tall, block_rows, depth).transpose(1, 0, 2, 3).reshape(panel, depth)
    at_col = lane // col_width == col_place
    gram_placed = jnp.where(at_col, jnp.tile(gram_panel, (1, col_count)), 0.0)
    update_part = gram_placed - lax.dot_general(
        left_factor, chosen, (((1,), (1,)), ((), ())), preferred_element_type=jnp.float32
    )
    right_placed = jnp.where(at_col, jnp.tile(right_here.T, (1, col_count)), 0.0)
    product = right_placed - lax.dot_general(
        solved_here, chosen, (((0,), (1,)), ((), ())), preferred_element_type=jnp.float32
    )

    diag_row = collect(diag_z[:kept], "row", row_count)
    other = lax.ppermute(diag_row, "col", [(i, i ^ 1) for i in range(col_count)])
    update = lax.psum_scatter(update_part, "col", scatter_dimension=0, tiled=True)
    product = product.reshape(col_count, vox_part // col_count, panel)
    product, _ = lax.optimization_barrier((product, diag_row))
    spread_out = lax.all_to_all(product, "col", 0, 0)

    factored = factor((col_place % 2).reshape(1), diag_row, other, panel)
    factored, spread_out, update = lax.optimization_barrier((factored, spread_out, update))
    rows_out, vox_out = forward(factored, update, jnp.sum(spread_out, axis=0))

    vox_out = vox_out.reshape(-1, row_count, block_rows).transpose(1, 0, 2)
    vox_out = lax.all_to_all(vox_out, "row", 0, 0)
    start = col_place * spread // col_count * (row_count // spread)
    vox_out = lax.dynamic_slice_in_dim(jnp.concatenate([vox_out, vox_out], axis=0), start, row_count, 0)
    rows_out = rows_out.reshape(-1, col_count, col_width).transpose(1, 0, 2)
    count = rows_out.shape[1] * col_width
    both = jnp.concatenate([rows_out.reshape(col_count, count), vox_out.reshape(col_count, -1)], axis=1)
    both = lax.all_to_all(both.reshape(col_count, -1, 128), "col", 0, 0).reshape(col_count, -1)
    panel_factor = both[:, :count].reshape(-1, col_width)
    vox_out = both[:, count:].reshape(col_count, per_col, -1, block_rows).transpose(1, 0, 2, 3)
    solved_panel = vox_out.reshape(vox, block_rows).T
    return (panel_factor, solved_panel)


def solution(mesh):
    in_specs = (P("row", "col"), P("row", "col"), P("row", "col"), P("row", "col"))
    out_specs = (P("row", "col"), P("row", "col"))
    return jax.shard_map(body, mesh=mesh, in_specs=in_specs, out_specs=out_specs, check_vma=False)
```

```python
import jax
import jax.numpy as jnp
from jax import lax
from jax.experimental import pallas as pl
from jax.experimental.pallas import tpu as pltpu
from jax.sharding import PartitionSpec as P

HI = lax.Precision.HIGHEST


def factor_block(s_ref, c_ref):
    lane = lax.broadcasted_iota(jnp.int32, (8, 128), 1)
    sub = lax.broadcasted_iota(jnp.int32, (8, 128), 0)

    def wide(value, at):
        return jnp.broadcast_to(value[:, at:at + 1], (8, 128))

    def apply(v, base, q):
        rows = s_ref[8 * v:8 * v + 8, :]
        part = [wide(rows, base + j) * q[j] for j in range(8)]
        total = ((part[0] + part[1]) + (part[2] + part[3])) + ((part[4] + part[5]) + (part[6] + part[7]))
        rows = jnp.where((lane >= base) & (lane < base + 8), 0.0, rows) - total
        s_ref[8 * v:8 * v + 8, :] = rows
        return rows

    w = s_ref[0:8, :]
    follow = s_ref[8:16, :]
    waiting = []
    for g in range(16):
        base = 8 * g
        inside = (lane >= base) & (lane < base + 8)
        x = [[None] * 8 for _ in range(8)]
        for j in range(8):
            c = wide(w, base + j)
            at = 72 * (g % 2) + 8 * j
            c_ref[at:at + 8, :] = c
            for i in range(j, 8):
                x[i][j] = c_ref[pl.ds(at + i, 8, stride=0), :]
        start = jnp.where(lane == sub + base, 1.0, jnp.where(inside, 0.0, w))
        at = 72 * (g % 2) + 64
        c_ref[at:at + 8, :] = start
        r = [c_ref[pl.ds(at + j, 8, stride=0), :] for j in range(8)]
        if g < 15:
            if waiting:
                follow = waiting.pop(0)()
            b = [wide(follow, base + k) for k in range(8)]
            follow = jnp.where(inside, 0.0, follow)
        ahead = [[None] * 8 for _ in range(8)]
        top = None
        share = -(-len(waiting) // 8)
        for j in range(8):
            d = 1.0 / x[j][j]
            s = lax.rsqrt(x[j][j])
            t = r[j] * s
            top = t if top is None else jnp.where(sub == j, t, top)
            f = {i: x[i][j] * d for i in range(j + 1, 8)}
            for i in range(j + 1, 8):
                for k in range(j + 1, i + 1):
                    x[i][k] = x[i][k] - (x[i][j] * x[k][j]) * d if i == j + 1 else x[i][k] - f[i] * x[k][j]
            p = r[j] * d
            for i in range(j + 1, 8):
                r[i] = r[i] - x[i][j] * p
            if g < 15:
                follow = follow - b[j] * p
                for k in range(j + 1, 8):
                    b[k] = b[k] - b[j] * f[k]
            for i in range(j):
                r[i] = r[i] - ahead[i][j] * p
                for k in range(j + 1, 8):
                    ahead[i][k] = ahead[i][k] - ahead[i][j] * f[k]
            r[j] = p
            for k in range(j + 1, 8):
                ahead[j][k] = f[k]
            for _ in range(share):
                if waiting:
                    waiting.pop(0)()
        s_ref[base:base + 8, :] = top
        w = follow
        waiting = [lambda v=v, base=base, q=r: apply(v, base, q) for v in range(g + 2, 16)]
    rows = lax.broadcasted_iota(jnp.int32, (128, 128), 0)
    cols = lax.broadcasted_iota(jnp.int32, (128, 128), 1)
    s_ref[...] = jnp.where(cols <= rows, s_ref[...], 0.0)


def mm(a, b):
    return lax.dot_general(a, b, (((1,), (0,)), ((), ())), precision=HI, preferred_element_type=jnp.float32)


def mtm(a, b):
    return lax.dot_general(a, b, (((0,), (0,)), ((), ())), precision=HI, preferred_element_type=jnp.float32)


def mmt(a, b):
    return lax.dot_general(a, b, (((1,), (1,)), ((), ())), precision=HI, preferred_element_type=jnp.float32)


def factor_kernel(core_ref, mine_ref, other_ref, out_ref, w_ref, s_ref, m_ref, c_ref, sems):
    big, n, _ = w_ref.shape
    rows, kept, half, lanes = mine_ref.shape
    tall = n // lanes
    wide = rows // tall
    core = core_ref[0]
    for y in range(tall):
        for d in range(kept):
            z = y - d
            if z < 0 and d * 2 >= tall:
                continue
            for x in range(wide):
                at = (wide * max(z, 0) + x) * 2 * half
                first = pl.ds(pl.multiple_of(at + core * half, half), half)
                second = pl.ds(pl.multiple_of(at + (1 - core) * half, half), half)
                if z >= 0:
                    cols = slice((y % 2) * lanes, (y % 2) * lanes + lanes)
                    w_ref[y // 2, first, cols] = mine_ref[wide * y + x, d]
                    w_ref[y // 2, second, cols] = other_ref[wide * y + x, d]
                else:
                    s_ref[first, :] = mine_ref[wide * y + x, d]
                    s_ref[second, :] = other_ref[wide * y + x, d]
            if z < 0:
                z += tall
                cols = slice((z % 2) * lanes, (z % 2) * lanes + lanes)
                w_ref[z // 2, y * lanes:(y + 1) * lanes, cols] = s_ref[...].T

    def step(b, carry):
        top = pl.multiple_of(b * 256, 256)
        mid = pl.multiple_of(b * 256 + 128, 128)

        def half_step(h, carry):
            @pl.when(h == 0)
            def _():
                s_ref[...] = w_ref[b, pl.ds(top, 128), 0:128]

            @pl.when(h == 1)
            def _():
                m_ref[0:128, 0:128] = s_ref[...]
                upper = mm(s_ref[...], w_ref[b, pl.ds(top, 128), 128:256])
                m_ref[0:128, 128:256] = upper
                s_ref[...] = w_ref[b, pl.ds(mid, 128), 128:256] - mtm(upper, upper)

            factor_block(s_ref, c_ref)
            return carry

        lax.fori_loop(0, 2, half_step, 0)
        lower = mtm(m_ref[0:128, 128:256], m_ref[0:128, 0:128])
        m_ref[128:256, 0:128] = -mm(s_ref[...], lower)
        m_ref[0:128, 128:256] = jnp.zeros((128, 128), jnp.float32)
        m_ref[128:256, 128:256] = s_ref[...]
        w_ref[b, pl.ds(top, 256), :] = m_ref[...]

        for j in range(1, big):
            @pl.when(j > b)
            def _():
                w_ref[j, pl.ds(top, 256), :] = mm(m_ref[...], w_ref[j, pl.ds(top, 256), :])

        for j in range(big):
            @pl.when(j >= b)
            def _():
                pltpu.make_async_copy(
                    w_ref.at[j, pl.ds(top, 256), :], out_ref.at[j, pl.ds(top, 256), :], sems.at[b, j]
                ).start()

        def below(i, carry):
            at = pl.multiple_of(i * 256, 256)
            for j in range(1, big):
                @pl.when(j >= i)
                def _():
                    w_ref[j, pl.ds(at, 256), :] = w_ref[j, pl.ds(at, 256), :] - mtm(
                        w_ref[i, pl.ds(top, 256), :], w_ref[j, pl.ds(top, 256), :]
                    )
            return carry

        lax.fori_loop(b + 1, big, below, 0)
        return carry

    lax.fori_loop(0, big, step, 0)
    for b in range(big):
        span = pl.ds(256 * b, 256)
        for j in range(b, big):
            pltpu.make_async_copy(w_ref.at[j, span, :], out_ref.at[j, span, :], sems.at[b, j]).wait()


def solve_kernel(from_ref, u_ref, v_ref, out_u_ref, out_v_ref, w_ref, x_ref, sems):
    big = w_ref.shape[0]
    n = u_ref.shape[0]
    copies = {}
    for b in range(big):
        span = pl.ds(256 * b, 256)
        for j in range(b, big):
            copies[b, j] = pltpu.make_async_copy(from_ref.at[j, span, :], w_ref.at[j, span, :], sems.at[b, j])
            copies[b, j].start()
    x_ref[0:n, :] = u_ref[...]
    x_ref[n:, :] = v_ref[...]
    for b in range(big):
        span = slice(256 * b, 256 * b + 256)
        copies[b, b].wait()
        y = mmt(x_ref[:, span], w_ref[b, span, :])
        out_u_ref[:, span] = y[0:n, :]
        out_v_ref[:, span] = y[n:, :]
        for j in range(b + 1, big):
            right = slice(256 * j, 256 * j + 256)
            copies[b, j].wait()
            x_ref[:, right] = x_ref[:, right] - mm(y, w_ref[j, span, :])


def factor(core, mine, other, panel):
    vmem = pl.BlockSpec(memory_space=pltpu.VMEM)
    big = panel // 256
    return pl.pallas_call(
        factor_kernel,
        out_shape=pltpu.HBM((big, panel, 256), jnp.float32),
        in_specs=[pl.BlockSpec(memory_space=pltpu.SMEM), vmem, vmem],
        out_specs=pl.BlockSpec(memory_space=pltpu.HBM),
        scratch_shapes=[
            pltpu.VMEM((big, panel, 256), jnp.float32),
            pltpu.VMEM((128, 128), jnp.float32),
            pltpu.VMEM((256, 256), jnp.float32),
            pltpu.VMEM((144, 128), jnp.float32),
            pltpu.SemaphoreType.DMA((big, big)),
        ],
        compiler_params=pltpu.CompilerParams(vmem_limit_bytes=16 * 1024 * 1024),
        cost_estimate=pl.CostEstimate(flops=panel**3, transcendentals=0, bytes_accessed=8 * panel * panel),
    )(core, mine, other)


def forward(w, u, v):
    vmem = pl.BlockSpec(memory_space=pltpu.VMEM)
    return pl.pallas_call(
        solve_kernel,
        out_shape=[jax.ShapeDtypeStruct(u.shape, jnp.float32), jax.ShapeDtypeStruct(v.shape, jnp.float32)],
        in_specs=[pl.BlockSpec(memory_space=pltpu.HBM), vmem, vmem],
        out_specs=[vmem, vmem],
        scratch_shapes=[
            pltpu.VMEM(w.shape, jnp.float32),
            pltpu.VMEM((u.shape[0] + v.shape[0], u.shape[1]), jnp.float32),
            pltpu.SemaphoreType.DMA((w.shape[0], w.shape[0])),
        ],
        compiler_params=pltpu.CompilerParams(vmem_limit_bytes=12 * 1024 * 1024),
    )(pltpu.with_memory_space_constraint(w, pltpu.HBM), u, v)


def split_three(value):
    high = lax.reduce_precision(value, 8, 7)
    rest = value - high
    middle = lax.reduce_precision(rest, 8, 7)
    return [part.astype(jnp.bfloat16) for part in (high, middle, rest - middle)]


def collect(value, axis, count, groups=None):
    many = jnp.broadcast_to(value[None], (count,) + value.shape)
    return lax.all_to_all(many, axis, 0, 0, axis_index_groups=groups)


def body(gram_panel, left_factor, solved_prev, right_block):
    row_count = lax.axis_size("row")
    col_count = lax.axis_size("col")
    row_place = lax.axis_index("row")
    col_place = lax.axis_index("col")
    block_rows = right_block.shape[0]
    col_width = gram_panel.shape[1]
    panel = block_rows * row_count
    depth = left_factor.shape[1]
    wide = 4
    tall = row_count // wide
    chips = col_count // 2
    x_place = row_place % wide
    along_x = [[y * wide + x for x in range(wide)] for y in range(tall)]
    along_y = [[y * wide + x for y in range(tall)] for x in range(wide)]
    along_z = [[z * 2 + core for z in range(chips)] for core in range(2)]
    own = left_factor[:block_rows]
    per_col = row_count // col_count
    lane = lax.broadcasted_iota(jnp.int32, (1, panel), 1)

    prev_rows, vox = solved_prev.shape
    vox_part = vox // per_col
    packed = jnp.concatenate([solved_prev] + split_three(right_block), axis=0)
    spread = 2
    piece_vox = vox_part // spread
    sends = []
    routes = []
    for turn in range(per_col):
        half = (row_place + turn) % per_col
        for q in range(spread):
            sends.append(lax.dynamic_slice_in_dim(packed, half * vox_part + q * piece_vox, piece_vox, 1))
            pairs = []
            for r in range(row_count):
                for c in range(col_count):
                    to_row = per_col * c + (r + turn) % per_col + q * (row_count // spread)
                    pairs.append((r * col_count + c, to_row % row_count * col_count + r // per_col))
            routes.append(pairs)
    own, *sends = lax.optimization_barrier((own, *sends))
    parts = [lax.ppermute(sent, ("row", "col"), pairs) for sent, pairs in zip(sends[:spread], routes[:spread])]
    from_y, *parts = lax.optimization_barrier((collect(own, "row", tall, along_y), *parts))
    packed = jnp.concatenate([own] + split_three(gram_panel[:block_rows]), axis=1)
    packed, from_y = lax.optimization_barrier((packed, from_y))
    from_x = collect(packed, "row", wide, along_x)
    rows_x = from_x[:, :, :depth].reshape(wide * block_rows, depth)
    rows_y = from_y.reshape(tall * block_rows, depth)
    gram_x = from_x[:, :, depth:].astype(jnp.float32).reshape(wide * block_rows, 3, per_col, block_rows)
    gram_x = gram_x[:, 0] + gram_x[:, 1] + gram_x[:, 2]
    per_x = wide // per_col
    gram_own = lax.dynamic_index_in_dim(gram_x, x_place % per_col, 1, keepdims=False)
    has_gram = (col_place % per_x) == (x_place // per_col)
    y_at = lax.broadcasted_iota(jnp.int32, (tall, 1, 1), 0)
    placed = jnp.where(has_gram & (y_at == col_place // per_x), gram_own.T[None], 0.0)
    partial = placed.reshape(tall * block_rows, wide * block_rows) - lax.dot_general(
        rows_y, rows_x, (((1,), (1,)), ((), ())), preferred_element_type=jnp.float32
    )
    kept = tall // 2 + 1
    turned = partial.reshape(tall, block_rows, wide * block_rows)[::-1]
    turned = lax.dynamic_slice_in_dim(jnp.concatenate([turned, turned], axis=0), tall - 1 - row_place // wide, tall, 0)
    thin = tall * block_rows // col_count
    partial = turned.reshape(col_count, thin, wide * block_rows)
    own_diag = jnp.sum(lax.all_to_all(partial, "col", 0, 0), axis=0)
    diag_z = collect(own_diag, "col", chips, along_z)

    chosen = lax.all_gather(rows_y, "row", axis=0, tiled=False, axis_index_groups=along_x)
    diag_z, chosen, *late = lax.optimization_barrier((diag_z[:kept], chosen, *sends[spread:]))
    chosen = chosen.reshape(wide, tall, block_rows, depth).transpose(1, 0, 2, 3).reshape(panel, depth)
    at_col = lane // col_width == col_place
    gram_placed = jnp.where(at_col, jnp.tile(gram_panel, (1, col_count)), 0.0)
    update_part = gram_placed - lax.dot_general(
        left_factor, chosen, (((1,), (1,)), ((), ())), preferred_element_type=jnp.float32
    )
    late = [lax.ppermute(sent, ("row", "col"), pairs) for sent, pairs in zip(late, routes[spread:])]
    diag_row, *late = lax.optimization_barrier((collect(diag_z, "row", row_count), *late))
    parts += late
    pieces = [jnp.concatenate(parts[turn * spread:(turn + 1) * spread], axis=1) for turn in range(per_col)]
    flip = (row_place % per_col) == 1
    first = jnp.where(flip, pieces[1], pieces[0])
    second = jnp.where(flip, pieces[0], pieces[1])
    solved_here = jnp.concatenate([first[:prev_rows], second[:prev_rows]], axis=0)
    right_here = jnp.concatenate([first[prev_rows:], second[prev_rows:]], axis=0).astype(jnp.float32)
    right_here = right_here.reshape(per_col, 3, block_rows, vox_part)
    right_here = (right_here[:, 0] + right_here[:, 1] + right_here[:, 2]).reshape(col_width, vox_part)
    right_placed = jnp.where(at_col, jnp.tile(right_here.T, (1, col_count)), 0.0)
    product = right_placed - lax.dot_general(
        solved_here, chosen, (((0,), (1,)), ((), ())), preferred_element_type=jnp.float32
    )

    other = lax.ppermute(diag_row, "col", [(i, i ^ 1) for i in range(col_count)])
    update = lax.psum_scatter(update_part, "col", scatter_dimension=0, tiled=True)
    product = product.reshape(col_count, vox_part // col_count, panel)
    product, _ = lax.optimization_barrier((product, diag_row))
    spread_out = lax.all_to_all(product, "col", 0, 0)

    factored = factor((col_place % 2).reshape(1), diag_row, other, panel)
    factored, spread_out, update = lax.optimization_barrier((factored, spread_out, update))
    rows_out, vox_out = forward(factored, update, jnp.sum(spread_out, axis=0))

    vox_out = vox_out.reshape(-1, row_count, block_rows).transpose(1, 0, 2)
    vox_out = lax.all_to_all(vox_out, "row", 0, 0)
    start = col_place * spread // col_count * (row_count // spread)
    vox_out = lax.dynamic_slice_in_dim(jnp.concatenate([vox_out, vox_out], axis=0), start, row_count, 0)
    rows_out = rows_out.reshape(-1, col_count, col_width).transpose(1, 0, 2)
    count = rows_out.shape[1] * col_width
    both = jnp.concatenate([rows_out.reshape(col_count, count), vox_out.reshape(col_count, -1)], axis=1)
    both = lax.all_to_all(both.reshape(col_count, -1, 128), "col", 0, 0).reshape(col_count, -1)
    panel_factor = both[:, :count].reshape(-1, col_width)
    vox_out = both[:, count:].reshape(col_count, per_col, -1, block_rows).transpose(1, 0, 2, 3)
    solved_panel = vox_out.reshape(vox, block_rows).T
    return (panel_factor, solved_panel)


def solution(mesh):
    in_specs = (P("row", "col"), P("row", "col"), P("row", "col"), P("row", "col"))
    out_specs = (P("row", "col"), P("row", "col"))
    return jax.shard_map(body, mesh=mesh, in_specs=in_specs, out_specs=out_specs, check_vma=False)
```

```python
import jax
import jax.numpy as jnp
from jax import lax
from jax.experimental import pallas as pl
from jax.experimental.pallas import tpu as pltpu
from jax.sharding import PartitionSpec as P

HI = lax.Precision.HIGHEST


def factor_block(s_ref, c_ref):
    lane = lax.broadcasted_iota(jnp.int32, (8, 128), 1)
    sub = lax.broadcasted_iota(jnp.int32, (8, 128), 0)

    def wide(value, at):
        return jnp.broadcast_to(value[:, at:at + 1], (8, 128))

    def apply(v, base, q):
        rows = s_ref[8 * v:8 * v + 8, :]
        part = [wide(rows, base + j) * q[j] for j in range(8)]
        total = ((part[0] + part[1]) + (part[2] + part[3])) + ((part[4] + part[5]) + (part[6] + part[7]))
        rows = jnp.where((lane >= base) & (lane < base + 8), 0.0, rows) - total
        s_ref[8 * v:8 * v + 8, :] = rows
        return rows

    w = s_ref[0:8, :]
    follow = s_ref[8:16, :]
    waiting = []
    for g in range(16):
        base = 8 * g
        inside = (lane >= base) & (lane < base + 8)
        x = [[None] * 8 for _ in range(8)]
        for j in range(8):
            c = wide(w, base + j)
            at = 72 * (g % 2) + 8 * j
            c_ref[at:at + 8, :] = c
            for i in range(j, 8):
                x[i][j] = c_ref[pl.ds(at + i, 8, stride=0), :]
        start = jnp.where(lane == sub + base, 1.0, jnp.where(inside, 0.0, w))
        at = 72 * (g % 2) + 64
        c_ref[at:at + 8, :] = start
        r = [c_ref[pl.ds(at + j, 8, stride=0), :] for j in range(8)]
        if g < 15:
            if waiting:
                follow = waiting.pop(0)()
            b = [wide(follow, base + k) for k in range(8)]
            follow = jnp.where(inside, 0.0, follow)
        ahead = [[None] * 8 for _ in range(8)]
        top = None
        share = -(-len(waiting) // 8)
        for j in range(8):
            d = 1.0 / x[j][j]
            s = lax.rsqrt(x[j][j])
            t = r[j] * s
            top = t if top is None else jnp.where(sub == j, t, top)
            f = {i: x[i][j] * d for i in range(j + 1, 8)}
            for i in range(j + 1, 8):
                for k in range(j + 1, i + 1):
                    x[i][k] = x[i][k] - (x[i][j] * x[k][j]) * d if i == j + 1 else x[i][k] - f[i] * x[k][j]
            p = r[j] * d
            for i in range(j + 1, 8):
                r[i] = r[i] - x[i][j] * p
            if g < 15:
                follow = follow - b[j] * p
                for k in range(j + 1, 8):
                    b[k] = b[k] - b[j] * f[k]
            for i in range(j):
                r[i] = r[i] - ahead[i][j] * p
                for k in range(j + 1, 8):
                    ahead[i][k] = ahead[i][k] - ahead[i][j] * f[k]
            r[j] = p
            for k in range(j + 1, 8):
                ahead[j][k] = f[k]
            for _ in range(share):
                if waiting:
                    waiting.pop(0)()
        s_ref[base:base + 8, :] = top
        w = follow
        waiting = [lambda v=v, base=base, q=r: apply(v, base, q) for v in range(g + 2, 16)]
    rows = lax.broadcasted_iota(jnp.int32, (128, 128), 0)
    cols = lax.broadcasted_iota(jnp.int32, (128, 128), 1)
    s_ref[...] = jnp.where(cols <= rows, s_ref[...], 0.0)


def mm(a, b):
    return lax.dot_general(a, b, (((1,), (0,)), ((), ())), precision=HI, preferred_element_type=jnp.float32)


def mtm(a, b):
    return lax.dot_general(a, b, (((0,), (0,)), ((), ())), precision=HI, preferred_element_type=jnp.float32)


def mmt(a, b):
    return lax.dot_general(a, b, (((1,), (1,)), ((), ())), precision=HI, preferred_element_type=jnp.float32)


def factor_kernel(core_ref, mine_ref, other_ref, out_ref, w_ref, s_ref, m_ref, c_ref, sems):
    big, n, _ = w_ref.shape
    rows, kept, half, lanes = mine_ref.shape
    tall = n // lanes
    wide = rows // tall
    core = core_ref[0]
    for y in range(tall):
        for d in range(kept):
            z = y - d
            if z < 0 and d * 2 >= tall:
                continue
            for x in range(wide):
                at = (wide * max(z, 0) + x) * 2 * half
                first = pl.ds(pl.multiple_of(at + core * half, half), half)
                second = pl.ds(pl.multiple_of(at + (1 - core) * half, half), half)
                if z >= 0:
                    cols = slice((y % 2) * lanes, (y % 2) * lanes + lanes)
                    w_ref[y // 2, first, cols] = mine_ref[wide * y + x, d]
                    w_ref[y // 2, second, cols] = other_ref[wide * y + x, d]
                else:
                    s_ref[first, :] = mine_ref[wide * y + x, d]
                    s_ref[second, :] = other_ref[wide * y + x, d]
            if z < 0:
                z += tall
                cols = slice((z % 2) * lanes, (z % 2) * lanes + lanes)
                w_ref[z // 2, y * lanes:(y + 1) * lanes, cols] = s_ref[...].T

    def step(b, carry):
        top = pl.multiple_of(b * 256, 256)
        mid = pl.multiple_of(b * 256 + 128, 128)

        def half_step(h, carry):
            @pl.when(h == 0)
            def _():
                s_ref[...] = w_ref[b, pl.ds(top, 128), 0:128]

            @pl.when(h == 1)
            def _():
                m_ref[0:128, 0:128] = s_ref[...]
                upper = mm(s_ref[...], w_ref[b, pl.ds(top, 128), 128:256])
                m_ref[0:128, 128:256] = upper
                s_ref[...] = w_ref[b, pl.ds(mid, 128), 128:256] - mtm(upper, upper)

            factor_block(s_ref, c_ref)
            return carry

        lax.fori_loop(0, 2, half_step, 0)
        lower = mtm(m_ref[0:128, 128:256], m_ref[0:128, 0:128])
        m_ref[128:256, 0:128] = -mm(s_ref[...], lower)
        m_ref[0:128, 128:256] = jnp.zeros((128, 128), jnp.float32)
        m_ref[128:256, 128:256] = s_ref[...]
        w_ref[b, pl.ds(top, 256), :] = m_ref[...]

        for j in range(1, big):
            @pl.when(j > b)
            def _():
                w_ref[j, pl.ds(top, 256), :] = mm(m_ref[...], w_ref[j, pl.ds(top, 256), :])

        for j in range(big):
            @pl.when(j >= b)
            def _():
                pltpu.make_async_copy(
                    w_ref.at[j, pl.ds(top, 256), :], out_ref.at[j, pl.ds(top, 256), :], sems.at[b, j]
                ).start()

        def below(i, carry):
            at = pl.multiple_of(i * 256, 256)
            for j in range(1, big):
                @pl.when(j >= i)
                def _():
                    w_ref[j, pl.ds(at, 256), :] = w_ref[j, pl.ds(at, 256), :] - mtm(
                        w_ref[i, pl.ds(top, 256), :], w_ref[j, pl.ds(top, 256), :]
                    )
            return carry

        lax.fori_loop(b + 1, big, below, 0)
        return carry

    lax.fori_loop(0, big, step, 0)
    for b in range(big):
        span = pl.ds(256 * b, 256)
        for j in range(b, big):
            pltpu.make_async_copy(w_ref.at[j, span, :], out_ref.at[j, span, :], sems.at[b, j]).wait()


def solve_kernel(from_ref, u_ref, v_ref, out_u_ref, out_v_ref, w_ref, x_ref, sems):
    big = w_ref.shape[0]
    n = u_ref.shape[0]
    copies = {}
    for b in range(big):
        span = pl.ds(256 * b, 256)
        for j in range(b, big):
            copies[b, j] = pltpu.make_async_copy(from_ref.at[j, span, :], w_ref.at[j, span, :], sems.at[b, j])
            copies[b, j].start()
    x_ref[0:n, :] = u_ref[...]
    x_ref[n:, :] = v_ref[...]
    for b in range(big):
        span = slice(256 * b, 256 * b + 256)
        copies[b, b].wait()
        y = mmt(x_ref[:, span], w_ref[b, span, :])
        out_u_ref[:, span] = y[0:n, :]
        out_v_ref[:, span] = y[n:, :]
        for j in range(b + 1, big):
            right = slice(256 * j, 256 * j + 256)
            copies[b, j].wait()
            x_ref[:, right] = x_ref[:, right] - mm(y, w_ref[j, span, :])


def factor(core, mine, other, panel):
    vmem = pl.BlockSpec(memory_space=pltpu.VMEM)
    big = panel // 256
    return pl.pallas_call(
        factor_kernel,
        out_shape=pltpu.HBM((big, panel, 256), jnp.float32),
        in_specs=[pl.BlockSpec(memory_space=pltpu.SMEM), vmem, vmem],
        out_specs=pl.BlockSpec(memory_space=pltpu.HBM),
        scratch_shapes=[
            pltpu.VMEM((big, panel, 256), jnp.float32),
            pltpu.VMEM((128, 128), jnp.float32),
            pltpu.VMEM((256, 256), jnp.float32),
            pltpu.VMEM((144, 128), jnp.float32),
            pltpu.SemaphoreType.DMA((big, big)),
        ],
        compiler_params=pltpu.CompilerParams(vmem_limit_bytes=16 * 1024 * 1024),
        cost_estimate=pl.CostEstimate(flops=panel**3, transcendentals=0, bytes_accessed=8 * panel * panel),
    )(core, mine, other)


def forward(w, u, v):
    vmem = pl.BlockSpec(memory_space=pltpu.VMEM)
    return pl.pallas_call(
        solve_kernel,
        out_shape=[jax.ShapeDtypeStruct(u.shape, jnp.float32), jax.ShapeDtypeStruct(v.shape, jnp.float32)],
        in_specs=[pl.BlockSpec(memory_space=pltpu.HBM), vmem, vmem],
        out_specs=[vmem, vmem],
        scratch_shapes=[
            pltpu.VMEM(w.shape, jnp.float32),
            pltpu.VMEM((u.shape[0] + v.shape[0], u.shape[1]), jnp.float32),
            pltpu.SemaphoreType.DMA((w.shape[0], w.shape[0])),
        ],
        compiler_params=pltpu.CompilerParams(vmem_limit_bytes=12 * 1024 * 1024),
    )(pltpu.with_memory_space_constraint(w, pltpu.HBM), u, v)


def split_three(value):
    high = lax.reduce_precision(value, 8, 7)
    rest = value - high
    middle = lax.reduce_precision(rest, 8, 7)
    return [part.astype(jnp.bfloat16) for part in (high, middle, rest - middle)]


def collect(value, axis, count, groups=None):
    many = jnp.broadcast_to(value[None], (count,) + value.shape)
    return lax.all_to_all(many, axis, 0, 0, axis_index_groups=groups)


def body(gram_panel, left_factor, solved_prev, right_block):
    row_count = lax.axis_size("row")
    col_count = lax.axis_size("col")
    row_place = lax.axis_index("row")
    col_place = lax.axis_index("col")
    block_rows = right_block.shape[0]
    col_width = gram_panel.shape[1]
    panel = block_rows * row_count
    depth = left_factor.shape[1]
    wide = 4
    tall = row_count // wide
    chips = col_count // 2
    x_place = row_place % wide
    along_x = [[y * wide + x for x in range(wide)] for y in range(tall)]
    along_y = [[y * wide + x for y in range(tall)] for x in range(wide)]
    along_z = [[z * 2 + core for z in range(chips)] for core in range(2)]
    own = left_factor[:block_rows]
    per_col = row_count // col_count
    lane = lax.broadcasted_iota(jnp.int32, (1, panel), 1)

    prev_rows, vox = solved_prev.shape
    vox_part = vox // per_col
    packed = jnp.concatenate([solved_prev] + split_three(right_block), axis=0)
    spread = 2
    piece_vox = vox_part // spread
    sends = []
    routes = []
    for turn in range(per_col):
        half = (row_place + turn) % per_col
        for q in range(spread):
            sends.append(lax.dynamic_slice_in_dim(packed, half * vox_part + q * piece_vox, piece_vox, 1))
            pairs = []
            for r in range(row_count):
                for c in range(col_count):
                    to_row = per_col * c + (r + turn) % per_col + q * (row_count // spread)
                    pairs.append((r * col_count + c, to_row % row_count * col_count + r // per_col))
            routes.append(pairs)
    parts = [lax.ppermute(sent, ("row", "col"), pairs) for sent, pairs in zip(sends, routes)]
    from_y, *parts = lax.optimization_barrier((collect(own, "row", tall, along_y), *parts))
    packed = jnp.concatenate([own] + split_three(gram_panel[:block_rows]), axis=1)
    packed, from_y = lax.optimization_barrier((packed, from_y))
    from_x = collect(packed, "row", wide, along_x)
    pieces = [jnp.concatenate(parts[turn * spread:(turn + 1) * spread], axis=1) for turn in range(per_col)]
    flip = (row_place % per_col) == 1
    first = jnp.where(flip, pieces[1], pieces[0])
    second = jnp.where(flip, pieces[0], pieces[1])
    solved_here = jnp.concatenate([first[:prev_rows], second[:prev_rows]], axis=0)
    right_here = jnp.concatenate([first[prev_rows:], second[prev_rows:]], axis=0).astype(jnp.float32)
    right_here = right_here.reshape(per_col, 3, block_rows, vox_part)
    right_here = (right_here[:, 0] + right_here[:, 1] + right_here[:, 2]).reshape(col_width, vox_part)
    rows_x = from_x[:, :, :depth].reshape(wide * block_rows, depth)
    rows_y = from_y.reshape(tall * block_rows, depth)
    gram_x = from_x[:, :, depth:].astype(jnp.float32).reshape(wide * block_rows, 3, per_col, block_rows)
    gram_x = gram_x[:, 0] + gram_x[:, 1] + gram_x[:, 2]
    per_x = wide // per_col
    gram_own = lax.dynamic_index_in_dim(gram_x, x_place % per_col, 1, keepdims=False)
    has_gram = (col_place % per_x) == (x_place // per_col)
    y_at = lax.broadcasted_iota(jnp.int32, (tall, 1, 1), 0)
    placed = jnp.where(has_gram & (y_at == col_place // per_x), gram_own.T[None], 0.0)
    partial = placed.reshape(tall * block_rows, wide * block_rows) - lax.dot_general(
        rows_y, rows_x, (((1,), (1,)), ((), ())), preferred_element_type=jnp.float32
    )
    kept = tall // 2 + 1
    turned = partial.reshape(tall, block_rows, wide * block_rows)[::-1]
    turned = lax.dynamic_slice_in_dim(jnp.concatenate([turned, turned], axis=0), tall - 1 - row_place // wide, tall, 0)
    thin = tall * block_rows // col_count
    partial = turned.reshape(col_count, thin, wide * block_rows)
    own_diag = jnp.sum(lax.all_to_all(partial, "col", 0, 0), axis=0)
    diag_z = collect(own_diag, "col", chips, along_z)

    chosen = lax.all_gather(rows_y, "row", axis=0, tiled=False, axis_index_groups=along_x)
    chosen = chosen.reshape(wide, tall, block_rows, depth).transpose(1, 0, 2, 3).reshape(panel, depth)
    at_col = lane // col_width == col_place
    gram_placed = jnp.where(at_col, jnp.tile(gram_panel, (1, col_count)), 0.0)
    update_part = gram_placed - lax.dot_general(
        left_factor, chosen, (((1,), (1,)), ((), ())), preferred_element_type=jnp.float32
    )
    right_placed = jnp.where(at_col, jnp.tile(right_here.T, (1, col_count)), 0.0)
    product = right_placed - lax.dot_general(
        solved_here, chosen, (((0,), (1,)), ((), ())), preferred_element_type=jnp.float32
    )

    diag_row = collect(diag_z[:kept], "row", row_count)
    other = lax.ppermute(diag_row, "col", [(i, i ^ 1) for i in range(col_count)])
    update = lax.psum_scatter(update_part, "col", scatter_dimension=0, tiled=True)
    product = product.reshape(col_count, vox_part // col_count, panel)
    product, _ = lax.optimization_barrier((product, diag_row))
    spread_out = lax.all_to_all(product, "col", 0, 0)

    factored = factor((col_place % 2).reshape(1), diag_row, other, panel)
    factored, spread_out, update = lax.optimization_barrier((factored, spread_out, update))
    rows_out, vox_out = forward(factored, update, jnp.sum(spread_out, axis=0))

    vox_out = vox_out.reshape(-1, row_count, block_rows).transpose(1, 0, 2)
    vox_out = lax.all_to_all(vox_out, "row", 0, 0)
    start = col_place * spread // col_count * (row_count // spread)
    vox_out = lax.dynamic_slice_in_dim(jnp.concatenate([vox_out, vox_out], axis=0), start, row_count, 0)
    rows_out = rows_out.reshape(-1, col_count, col_width).transpose(1, 0, 2)
    count = rows_out.shape[1] * col_width
    both = jnp.concatenate([rows_out.reshape(col_count, count), vox_out.reshape(col_count, -1)], axis=1)
    both = lax.all_to_all(both.reshape(col_count, -1, 128), "col", 0, 0).reshape(col_count, -1)
    panel_factor = both[:, :count].reshape(-1, col_width)
    vox_out = both[:, count:].reshape(col_count, per_col, -1, block_rows).transpose(1, 0, 2, 3)
    solved_panel = vox_out.reshape(vox, block_rows).T
    return (panel_factor, solved_panel)


def solution(mesh):
    in_specs = (P("row", "col"), P("row", "col"), P("row", "col"), P("row", "col"))
    out_specs = (P("row", "col"), P("row", "col"))
    return jax.shard_map(body, mesh=mesh, in_specs=in_specs, out_specs=out_specs, check_vma=False)
```
